256 devices in a mesh: env: 32 (over x, z), cand: 8 (over y, core).
Axes of the slice: x: 4, y: 4, z: 8, core: 2. Of those that a mesh axis runs over, the one named last changes fastest.
Arguments:
- params: bfloat16 [346880], P(('env', 'cand')), may hold values from -6 to 6
- h_start: float32 [64, 200], P('env'), may hold values from -1 to 1
- z_start: float32 [64, 30], P('env'), may hold values from -5 to 5
- action_noise: bfloat16 [3, 12, 6, 64, 1024], P(None, None, None, 'env', 'cand'), may hold values from -4 to 4
- state_noise: bfloat16 [3, 12, 30, 64, 1024], P(None, None, None, 'env', 'cand'), may hold values from -4 to 4
- elites: int32 [3, 64, 100], P(None, 'env'), may hold values from 0 to 1023, as said below
Outputs:
- plan_mean: float32 [12, 6, 64], P(None, None, 'env')
- plan_spread: float32 [12, 6, 64], P(None, None, 'env')
- returns: float32 [3, 64, 1024], P(None, 'env', 'cand')
- best_return: float32 [3, 64], P(None, 'env')
The draws below stay inside these ranges and needn't reach their ends.
Inputs may be any that keep to these rules, and one draw needn't show every extreme that they name: `elites`: for each iteration and environment, 100 different candidate numbers.
All inputs are finite; a program needn't handle non-finite values.
Results may differ from the reference program's by a relative error of at most 0.0065.
Values may be sent and summed in bfloat16 or wider, within the bound.
No kernel may reach another device: no remote copies, remote signals or barrier semaphores. Data moves between devices by JAX's collectives and lax.ppermute only.
A program may use at most 64 MiB of HBM per device.

```python
import jax
import jax.numpy as jnp
from jax import lax

D_DET = 200
STOCH = 30
HID = 200
ACT = 6
HOR = 12
ITERS = 3
ELITE = 100
ENVS = 64
CANDS = 1024
PARAMS = 346880


def draw_elites(key, part):
    keys = jax.random.split(jax.random.fold_in(key, 17), ITERS * ENVS)

    def pick_one(single_key):
        return jax.random.permutation(single_key, jnp.arange(CANDS, dtype=jnp.int32))[:ELITE]
    picked = jax.vmap(pick_one)(keys)
    return picked.reshape(ITERS, ENVS, ELITE).astype(jnp.int32)


def level_of(stream_key, extent, shards, smallest, top_value):
    def one(position, blocks):
        steps = jax.random.uniform(jax.random.fold_in(jax.random.fold_in(stream_key, 6), position), (blocks,), jnp.float32, smallest / len(shards), top_value / len(shards))
        return jnp.repeat(jnp.exp(steps), extent[position] // blocks).reshape((-1,) + (1,) * (len(extent) - position - 1))

    gain = one(*shards[0])
    for cut in shards[1:]:
        gain = gain * one(*cut)
    return gain


def gaussian(key, dims, width, limit, shards=(), kind=jnp.bfloat16):
    entries = width * jax.random.normal(key, dims, jnp.float32)
    if shards:
        entries = entries * level_of(key, dims, shards, -0.22, 0.18)
    return jnp.clip(entries, -limit, limit).astype(kind)


def setup_inputs(seed: int = 0) -> dict:
    key_of = jax.random.split(jax.random.key(seed), 7)
    return {
        "params": gaussian(key_of[0], (PARAMS,), 1.0, 6.0, ((0, 256),)),
        "h_start": jnp.clip(jax.random.uniform(key_of[1], (ENVS, D_DET), jnp.float32, -1.0, 1.0) * level_of(key_of[1], (ENVS, D_DET), ((0, 32),), -0.4, 0.0), -1.0, 1.0),
        "z_start": gaussian(key_of[2], (ENVS, STOCH), 1.0, 5.0, ((0, 32),), jnp.float32),
        "action_noise": gaussian(key_of[3], (ITERS, HOR, ACT, ENVS, CANDS), 1.0, 4.0, ((3, 32), (4, 8))),
        "state_noise": gaussian(key_of[4], (ITERS, HOR, STOCH, ENVS, CANDS), 1.0, 4.0, ((3, 32), (4, 8))),
        "elites": draw_elites(jax.random.fold_in(key_of[6], 71), 0),
    }


bias_scale = 0.2
min_scale = 0.1
variance_floor = 1e-05

def split_params(flat_params):
    layer_shapes = [(STOCH + ACT, HID), (HID + D_DET, 2 * D_DET), (HID + D_DET, D_DET), (D_DET, HID), (HID, 2 * STOCH), (D_DET + STOCH, HID), (HID, 1)]
    offset = 0
    layers = []
    for fan_in, fan_out in layer_shapes:
        matrix = flat_params[offset:offset + fan_in * fan_out].reshape(fan_in, fan_out)
        offset = offset + fan_in * fan_out
        biases = flat_params[offset:offset + fan_out]
        offset = offset + fan_out
        layers.append((matrix.T, biases.astype(jnp.float32) * bias_scale, fan_in ** (-0.5)))
    return layers

def affine(layer, inputs):
    matrix_t, biases, factor = layer
    return jnp.dot(matrix_t, inputs, preferred_element_type=jnp.float32) * factor + biases[:, None]

def rollout(layers, start_state, start_latent, action_seq, noise_seq):

    def advance(carried, inputs):
        state, latent, return_sum = carried
        action, sample_noise = inputs
        joined = jnp.concatenate([latent, action], 0).astype(jnp.bfloat16)
        embedded = jax.nn.elu(affine(layers[0], joined)).astype(jnp.bfloat16)
        gate_values = jax.nn.sigmoid(affine(layers[1], jnp.concatenate([embedded, state.astype(jnp.bfloat16)], 0)))
        reset_gate = gate_values[:D_DET]
        update = gate_values[D_DET:]
        proposal = jnp.tanh(affine(layers[2], jnp.concatenate([embedded, (reset_gate * state).astype(jnp.bfloat16)], 0)))
        next_state = update * state + (1.0 - update) * proposal
        state_low = next_state.astype(jnp.bfloat16)
        prior_hidden = jax.nn.elu(affine(layers[3], state_low)).astype(jnp.bfloat16)
        prior_stats = affine(layers[4], prior_hidden)
        prior_scale = jax.nn.softplus(prior_stats[STOCH:]) + min_scale
        next_latent = prior_stats[:STOCH] + prior_scale * sample_noise.astype(jnp.float32)
        reward_hidden = jax.nn.elu(affine(layers[5], jnp.concatenate([state_low, next_latent.astype(jnp.bfloat16)], 0))).astype(jnp.bfloat16)
        reward = affine(layers[6], reward_hidden)[0]
        return ((next_state, next_latent, return_sum + reward), None)
    initial = (start_state, start_latent, jnp.zeros(start_state.shape[1], jnp.float32))
    final, _ = lax.scan(advance, initial, (action_seq, noise_seq))
    return final[2]

def reference(params, h_start, z_start, action_noise, state_noise, elites):
    layers = split_params(params)
    row_count = ENVS * CANDS
    start_state = jnp.broadcast_to(h_start.T[:, :, None], (D_DET, ENVS, CANDS)).reshape(D_DET, row_count)
    start_latent = jnp.broadcast_to(z_start.T[:, :, None], (STOCH, ENVS, CANDS)).reshape(STOCH, row_count)
    center = jnp.zeros((HOR, ACT, ENVS), jnp.float32)
    spread = jnp.ones((HOR, ACT, ENVS), jnp.float32)
    candidate_ids = jnp.arange(CANDS, dtype=jnp.int32)
    totals = []
    best_values = []
    for number in range(ITERS):
        actions = center[..., None] + spread[..., None] * action_noise[number].astype(jnp.float32)
        return_sum = rollout(layers, start_state, start_latent, actions.reshape(HOR, ACT, row_count), state_noise[number].reshape(HOR, STOCH, row_count))
        return_grid = return_sum.reshape(ENVS, CANDS)
        totals.append(return_grid)
        best_values.append(lax.optimization_barrier(jnp.max(return_grid, axis=1)))
        worst = lax.optimization_barrier(jnp.min(return_grid, axis=1))
        chosen = jnp.any(elites[number][:, :, None] == candidate_ids[None, None, :], axis=1).astype(jnp.float32)
        weight = chosen * (return_grid - worst[:, None] + 1.0)
        total = lax.optimization_barrier(jnp.sum(weight, axis=1))
        center = lax.optimization_barrier(jnp.sum(actions * weight[None, None], axis=3)) / total[None, None]
        deviation = actions - center[..., None]
        spread = jnp.sqrt(lax.optimization_barrier(jnp.sum(weight[None, None] * deviation * deviation, axis=3)) / total[None, None] + variance_floor)
    return (center, spread, jnp.stack(totals), jnp.stack(best_values))
```

```python
import functools

import jax
import jax.numpy as jnp
from jax import lax
from jax.experimental import pallas as pl
from jax.experimental.pallas import tpu as pltpu
from jax.sharding import PartitionSpec as P

D_DET = 200
STOCH = 30
HID = 200
ACT = 6
HOR = 12
ITERS = 3

PEERS = 8
ENVS_HERE = 2
CANDS_HERE = 128
COLS = ENVS_HERE * CANDS_HERE

WIDE = 208
DEEP = 256
ROWS = 96
ONE = 96

bias_scale = 0.2
min_scale = 0.1
variance_floor = 1e-05

S36, S400, S200, S230 = (float(n) ** -0.5 for n in (36, 400, 200, 230))
LOG2E = 1.4426950408889634

F32, BF16 = jnp.float32, jnp.bfloat16


def dot(a, b):
    return jnp.dot(a, b, preferred_element_type=F32)


def scaled_elu(y, scale):
    return jnp.where(y > 0, y * scale, jnp.exp2(y * (scale * LOG2E)) - 1.0)


def softplus(v):
    return jnp.maximum(v, 0.0) + jnp.log(1.0 + jnp.exp(-jnp.abs(v)))


def refit(state, gathered):
    rows = []
    best = []
    for e in range(ENVS_HERE):
        m1, c1, m2, c2 = (gathered[:, 4 * e + k, :] for k in range(4))
        lowest = c1[:, ONE + 2 : ONE + 3]
        highest = c1[:, ONE + 1 : ONE + 2]
        worst = jnp.min(lowest, axis=0, keepdims=True)
        best.append(jnp.max(highest, axis=0, keepdims=True))
        lift = lowest - worst
        m1 = jnp.sum(m1 + lift * c1, axis=0, keepdims=True)
        m2 = jnp.sum(m2 + lift * c2, axis=0, keepdims=True)
        total = m1[:, ONE : ONE + 1]
        m1 = m1 / total
        m2 = m2 / total
        center = state[2 * e : 2 * e + 1]
        spread = state[2 * e + 1 : 2 * e + 2]
        rows.append(center + spread * m1)
        rows.append(
            jnp.sqrt(spread * spread * jnp.maximum(m2 - m1 * m1, 0.0) + variance_floor)
        )
    state = jnp.concatenate(rows + [jnp.zeros((4, 128), F32)], 0)
    return state, jnp.concatenate([jnp.broadcast_to(b, (1, 128)) for b in best], 0)


def split(v):
    hi = v.astype(BF16)
    return hi, v - hi.astype(F32)


def rollout_kernel(
    first, number, w_h, w_x, w_za, w_r, w_p, w_7, h0, z0, a_noise, s_noise, chosen, *rest
):
    if first:
        ret_ref, msg_ref, acts, h_ref, q_ref = rest
    else:
        state_ref, got_ref, ret_ref, msg_ref, new_state_ref, best_ref, acts, h_ref, q_ref = rest
    noise = a_noise[number].astype(F32)
    if first:
        acts[...] = noise
    else:
        state, best = refit(state_ref[...], got_ref[...])
        new_state_ref[...] = state
        best_ref[...] = best
        columns = jnp.transpose(state)
        for e in range(ENVS_HERE):
            at = pl.ds(e * CANDS_HERE, CANDS_HERE)
            center = columns[:ROWS, 2 * e : 2 * e + 1]
            spread = columns[:ROWS, 2 * e + 1 : 2 * e + 2]
            acts[:, at] = center + spread * noise[:, e * CANDS_HERE : (e + 1) * CANDS_HERE]
    rows8 = lax.broadcasted_iota(jnp.int32, (8, COLS), 0)
    ones8 = jnp.where(rows8 < 2, 1.0, 0.0).astype(F32)
    ones48 = jnp.concatenate([ones8, jnp.zeros((DEEP - WIDE - 8, COLS), F32)], 0).astype(BF16)

    def deep(v):
        return jnp.concatenate([v.astype(BF16), ones48], 0)

    h_ref[...] = h0[...]
    q_ref[...] = jnp.zeros_like(q_ref)

    def step(t, z):
        h = h_ref[...]
        hd = deep(h)
        gates_h = dot(w_h[: 2 * WIDE], hd)
        za = jnp.concatenate([z, acts[pl.ds(pl.multiple_of(t * 8, 8), 8), :], ones8], 0).astype(BF16)
        x = deep(scaled_elu(dot(w_za[:WIDE], za), S36))
        gates = dot(w_x[: 2 * WIDE], x) + gates_h
        reset = jnp.tanh(gates[:WIDE] * (0.5 * S400))
        half = 0.5 * h
        rh = deep(half + reset * half)
        proposal = jnp.tanh((dot(w_x[2 * WIDE :], x) + dot(w_r[...], rh)) * S400)
        update = 0.5 + 0.5 * jnp.tanh(gates[WIDE:] * (0.5 * S400))
        h = proposal + update * (h - proposal)
        h_ref[...] = h
        hd = deep(h)
        p = deep(scaled_elu(dot(w_h[2 * WIDE : 3 * WIDE], hd), S200))
        s = dot(w_p[...], p) * S200
        scale = softplus(s[32:]) + min_scale
        z = s[:32] + scale * s_noise[number, t].astype(F32)
        zb = jnp.concatenate([z, jnp.zeros((16, COLS), F32)], 0).astype(BF16)
        q = scaled_elu(dot(w_h[3 * WIDE :], hd) + dot(w_za[WIDE:], zb), S230)
        q_ref[...] += q.astype(BF16).astype(F32)
        return z

    lax.fori_loop(0, HOR, step, z0[...])

    total = jnp.concatenate(
        [q_ref[...], ones8, jnp.zeros((DEEP - WIDE - 8, COLS), F32)], 0
    )
    returns = lax.dot(w_7[...], total, precision=lax.Precision.HIGHEST)
    lanes = lax.broadcasted_iota(jnp.int32, (1, 128), 1)
    rows16 = lax.broadcasted_iota(jnp.int32, (16, 128), 0)
    ones_row = jnp.where(lax.broadcasted_iota(jnp.int32, (32, CANDS_HERE), 0) == 0, 1.0, 0.0)
    out = []
    for e in range(ENVS_HERE):
        r = returns[0:1, e * CANDS_HERE : (e + 1) * CANDS_HERE]
        ret_ref[e : e + 1, :] = r
        lowest = jnp.min(r, axis=1, keepdims=True)
        highest = jnp.max(r, axis=1, keepdims=True)
        c = chosen[number, e : e + 1, :]
        w = c * (r - lowest + 1.0)
        hi, w1 = split(w)
        mid, w2 = split(w1)
        left = jnp.where(
            rows16 == 0,
            hi.astype(F32),
            jnp.where(rows16 == 1, mid.astype(F32), jnp.where(rows16 == 2, w2, jnp.where(rows16 == 3, c, 0.0))),
        ).astype(BF16)
        n = jnp.concatenate([noise[:, e * CANDS_HERE : (e + 1) * CANDS_HERE], ones_row], 0)
        n2_hi, n2_lo = split(n * n)
        right = jnp.concatenate([n.astype(BF16), n2_hi, n2_lo.astype(BF16)], 0)
        sums = lax.dot_general(left, right, (((1,), (1,)), ((), ())), preferred_element_type=F32)
        first_m, second_m = sums[:, :128], sums[:, 128:256] + sums[:, 256:]
        c1 = jnp.where(lanes == ONE + 1, highest, jnp.where(lanes == ONE + 2, lowest, first_m[3:4]))
        out += [
            first_m[0:1] + first_m[1:2] + first_m[2:3],
            c1,
            second_m[0:1] + second_m[1:2] + second_m[2:3],
            second_m[3:4],
        ]
    msg = jnp.concatenate(out, 0)
    for k in range(PEERS):
        msg_ref[k] = msg


def last_kernel(state_ref, got_ref, out_ref, best_ref):
    state, best = refit(state_ref[...], got_ref[...])
    out_ref[...] = jnp.transpose(state)
    best_ref[...] = best


VMEM = pl.BlockSpec(memory_space=pltpu.VMEM)


def rollout(number, weights, h0, z0, a_noise, s_noise, chosen, state, got):
    first = state is None
    shapes = [
        jax.ShapeDtypeStruct((ENVS_HERE, CANDS_HERE), F32),
        jax.ShapeDtypeStruct((PEERS, 8, 128), F32),
    ]
    args = [*weights, h0, z0, a_noise, s_noise, chosen]
    if not first:
        shapes += [
            jax.ShapeDtypeStruct((8, 128), F32),
            jax.ShapeDtypeStruct((ENVS_HERE, 128), F32),
        ]
        args += [state, got]
    return pl.pallas_call(
        functools.partial(rollout_kernel, first, number),
        out_shape=shapes,
        in_specs=[VMEM] * len(args),
        out_specs=[VMEM] * len(shapes),
        scratch_shapes=[
            pltpu.VMEM((ROWS, COLS), F32),
            pltpu.VMEM((WIDE, COLS), F32),
            pltpu.VMEM((WIDE, COLS), F32),
        ],
        compiler_params=pltpu.CompilerParams(vmem_limit_bytes=40 << 20),
        name=f"rollout_{number}",
    )(*args)


def prepared(flat):
    shapes = [(36, 200), (400, 400), (400, 200), (200, 200), (200, 60), (230, 200), (200, 1)]
    offset = 0
    mats, biases = [], []
    for fan_in, fan_out in shapes:
        mats.append(flat[offset : offset + fan_in * fan_out].reshape(fan_in, fan_out).T)
        offset += fan_in * fan_out
        b = flat[offset : offset + fan_out].astype(F32) * (bias_scale * fan_in**0.5)
        hi = b.astype(BF16)
        biases.append(jnp.stack([hi, (b - hi.astype(F32)).astype(BF16)], 1))
        offset += fan_out

    def pad(a, rows, cols):
        return jnp.pad(a, ((0, rows - a.shape[0]), (0, cols - a.shape[1])))

    def biased(a, b, rows=WIDE):
        return pad(jnp.concatenate([pad(a, a.shape[0], WIDE), b], 1), rows, DEEP)

    m1, m2, m3, m4, m5, m6, m7 = mats
    b1, b2, b3, b4, b5, b6, b7 = biases
    w_h = jnp.concatenate(
        [
            pad(m2[:200, 200:], WIDE, DEEP),
            pad(m2[200:, 200:], WIDE, DEEP),
            biased(m4, b4),
            biased(m6[:, :200], b6),
        ],
        0,
    )
    w_x = jnp.concatenate(
        [biased(m2[:200, :200], b2[:200]), biased(m2[200:, :200], b2[200:]), biased(m3[:, :200], b3)],
        0,
    )
    w_za = jnp.concatenate(
        [
            pad(jnp.concatenate([pad(m1[:, :30], 200, 32), pad(m1[:, 30:], 200, 8), b1], 1), WIDE, 48),
            pad(m6[:, 200:], WIDE, 48),
        ],
        0,
    )
    w_r = pad(m3[:, 200:], WIDE, DEEP)
    w_p = jnp.concatenate([biased(m5[:30], b5[:30], 32), biased(m5[30:], b5[30:], 32)], 0)
    last_bias = HOR * S200 * (b7[:, 0:1].astype(F32) + b7[:, 1:2].astype(F32))
    w_7 = pad(jnp.concatenate([pad(m7.astype(F32) * S200, 1, WIDE), last_bias], 1), 8, DEEP)
    return w_h, w_x, w_za, w_r, w_p, w_7


def from_peers(block, axis, peers, groups=None):
    return lax.all_to_all(
        jnp.broadcast_to(block[None], (peers, *block.shape)),
        axis,
        0,
        0,
        tiled=True,
        axis_index_groups=groups,
    )


def gathered_params(shard):
    size = shard.shape[0]
    block = jnp.pad(shard, (0, 2048 - size)).reshape(16, 128)
    block = from_peers(block, "env", 32)
    along_y = [[c, 2 + c, 4 + c, 6 + c] for c in range(2)]
    block = from_peers(block, "cand", 4, along_y)
    other = lax.ppermute(block, "cand", [(i, i ^ 1) for i in range(8)])
    low = lax.axis_index("cand") % 2 == 0
    both = jnp.stack([jnp.where(low, block, other), jnp.where(low, other, block)])
    both = both.reshape(2, 4, 32, 2048)[..., :size]
    return both.transpose(2, 1, 0, 3).reshape(-1)


def body(params, h_start, z_start, action_noise, state_noise, elites):
    a_noise = jnp.pad(
        action_noise.reshape(ITERS, HOR, ACT, COLS), ((0, 0), (0, 0), (0, 8 - ACT), (0, 0))
    ).reshape(ITERS, ROWS, COLS)
    s_noise = jnp.pad(
        state_noise.reshape(ITERS, HOR, STOCH, COLS), ((0, 0), (0, 0), (0, 32 - STOCH), (0, 0))
    )

    def spread_out(v, rows):
        v = jnp.pad(v.T, ((0, rows - v.shape[1]), (0, 0)))
        return jnp.broadcast_to(v[:, :, None], (rows, ENVS_HERE, CANDS_HERE)).reshape(rows, COLS)

    h0 = spread_out(h_start, WIDE)
    z0 = spread_out(z_start, 32)
    ids = lax.axis_index("cand") * CANDS_HERE + jnp.arange(CANDS_HERE, dtype=jnp.int32)
    chosen = jnp.any(elites[:, :, :, None] == ids, axis=2).astype(F32)

    weights = prepared(gathered_params(params))
    rets, bests = [], []
    state = got = None
    for number in range(ITERS):
        out = rollout(number, weights, h0, z0, a_noise, s_noise, chosen, state, got)
        rets.append(out[0])
        if number == 0:
            state = jnp.broadcast_to(
                jnp.array([0.0, 1.0, 0.0, 1.0, 0.0, 0.0, 0.0, 0.0], F32)[:, None], (8, 128)
            )
        else:
            state = out[2]
            bests.append(out[3])
        got = lax.all_to_all(out[1], "cand", 0, 0, tiled=True)
    columns, best = pl.pallas_call(
        last_kernel,
        out_shape=[
            jax.ShapeDtypeStruct((128, 8), F32),
            jax.ShapeDtypeStruct((ENVS_HERE, 128), F32),
        ],
        in_specs=[VMEM] * 2,
        out_specs=[VMEM] * 2,
        name="last",
    )(state, got)
    bests.append(best)
    columns = columns[:ROWS].reshape(HOR, 8, 8)[:, :ACT]
    return (
        columns[:, :, 0:4:2],
        columns[:, :, 1:4:2],
        jnp.stack(rets),
        jnp.stack([b[:, 0] for b in bests]),
    )


def solution(mesh):
    placed = (
        P(("env", "cand")),
        P("env", None),
        P("env", None),
        P(None, None, None, "env", "cand"),
        P(None, None, None, "env", "cand"),
        P(None, "env", None),
    )
    return jax.shard_map(
        body,
        mesh=mesh,
        in_specs=placed,
        out_specs=(
            P(None, None, "env"),
            P(None, None, "env"),
            P(None, "env", "cand"),
            P(None, "env"),
        ),
        check_vma=False,
    )
```

```python
import functools

import jax
import jax.numpy as jnp
from jax import lax
from jax.experimental import pallas as pl
from jax.experimental.pallas import tpu as pltpu
from jax.sharding import PartitionSpec as P

D_DET = 200
STOCH = 30
HID = 200
ACT = 6
HOR = 12
ITERS = 3

PEERS = 8
ENVS_HERE = 2
CANDS_HERE = 128
COLS = ENVS_HERE * CANDS_HERE

WIDE = 208
DEEP = 256
ROWS = 96
ONE = 96

bias_scale = 0.2
min_scale = 0.1
variance_floor = 1e-05

S36, S400, S200, S230 = (float(n) ** -0.5 for n in (36, 400, 200, 230))
LOG2E = 1.4426950408889634

F32, BF16 = jnp.float32, jnp.bfloat16


def dot(a, b):
    return jnp.dot(a, b, preferred_element_type=F32)


def scaled_elu(y, scale):
    return jnp.where(y > 0, y * scale, jnp.exp2(y * (scale * LOG2E)) - 1.0)


def softplus(v):
    return jnp.maximum(v, 0.0) + jnp.log(1.0 + jnp.exp(-jnp.abs(v)))


def refit(state, gathered):
    rows = []
    best = []
    for e in range(ENVS_HERE):
        m1, c1, m2, c2 = (gathered[:, 4 * e + k, :] for k in range(4))
        lowest = c1[:, ONE + 2 : ONE + 3]
        highest = c1[:, ONE + 1 : ONE + 2]
        worst = jnp.min(lowest, axis=0, keepdims=True)
        best.append(jnp.max(highest, axis=0, keepdims=True))
        lift = lowest - worst
        m1 = jnp.sum(m1 + lift * c1, axis=0, keepdims=True)
        m2 = jnp.sum(m2 + lift * c2, axis=0, keepdims=True)
        total = m1[:, ONE : ONE + 1]
        m1 = m1 / total
        m2 = m2 / total
        center = state[2 * e : 2 * e + 1]
        spread = state[2 * e + 1 : 2 * e + 2]
        rows.append(center + spread * m1)
        rows.append(
            jnp.sqrt(spread * spread * jnp.maximum(m2 - m1 * m1, 0.0) + variance_floor)
        )
    state = jnp.concatenate(rows + [jnp.zeros((4, 128), F32)], 0)
    return state, jnp.concatenate([jnp.broadcast_to(b, (1, 128)) for b in best], 0)


def split(v):
    hi = v.astype(BF16)
    return hi, v - hi.astype(F32)


def rollout_kernel(
    first, number, w_h, w_x, w_1, w_5, w_6z, w_r, w_7, h0, z0, a_noise, s_noise, chosen, *rest
):
    if first:
        ret_ref, msg_ref, acts = rest
    else:
        state_ref, got_ref, ret_ref, msg_ref, new_state_ref, best_ref, acts = rest
    noise = a_noise[number].astype(F32)
    if first:
        acts[...] = noise
    else:
        state, best = refit(state_ref[...], got_ref[...])
        new_state_ref[...] = state
        best_ref[...] = best
        columns = jnp.transpose(state)
        for e in range(ENVS_HERE):
            at = pl.ds(e * CANDS_HERE, CANDS_HERE)
            center = columns[:ROWS, 2 * e : 2 * e + 1]
            spread = columns[:ROWS, 2 * e + 1 : 2 * e + 2]
            acts[:, at] = center + spread * noise[:, e * CANDS_HERE : (e + 1) * CANDS_HERE]
    ones8 = jnp.where(lax.broadcasted_iota(jnp.int32, (8, COLS), 0) < 2, 1.0, 0.0).astype(F32)
    filler = jnp.zeros((80, COLS), F32)
    in_latent = lax.broadcasted_iota(jnp.int32, (1, 128), 1) < 32

    def drawn(t, n):
        block = jnp.concatenate([n, acts[t * 8 : t * 8 + 8, :], ones8, filler], 0)
        return jnp.transpose(block)

    def spread_out(ref):
        return jnp.concatenate(
            [jnp.broadcast_to(ref[e : e + 1, :], (CANDS_HERE, ref.shape[1])) for e in range(ENVS_HERE)], 0
        )

    h = spread_out(h0)
    q_sum = None
    for t in range(HOR + 1):
        hd = h.astype(BF16)
        if t == 0:
            za = (spread_out(z0) + drawn(0, jnp.zeros((32, COLS), F32))).astype(BF16)
        else:
            p = scaled_elu(dot(hd, w_h[:, 512:768]), S200).astype(BF16)
            s = dot(p, w_5[...]) * S200
            scale = jnp.where(in_latent, softplus(s[:, 128:]) + min_scale, 1.0)
            n = s_noise[number, t - 1].astype(F32)
            za = (s[:, :128] + scale * drawn(min(t, HOR - 1), n)).astype(BF16)
            q = scaled_elu(dot(hd, w_h[:, 768:]) + dot(za, w_6z[...]), S230)
            q = q.astype(BF16).astype(F32)
            q_sum = q if q_sum is None else q_sum + q
        if t == HOR:
            break
        x = scaled_elu(dot(za, w_1[...]), S36).astype(BF16)
        gates = dot(x, w_x[:, :512]) + dot(hd, w_h[:, :512])
        half = 0.5 * h
        rh = (half + jnp.tanh(gates[:, :256] * (0.5 * S400)) * half).astype(BF16)
        update = 0.5 + 0.5 * jnp.tanh(gates[:, 256:] * (0.5 * S400))
        proposal = jnp.tanh((dot(x, w_x[:, 512:]) + dot(rh, w_r[...])) * S400)
        h = proposal + update * (h - proposal)

    returns = lax.dot_general(
        w_7[...], q_sum, (((1,), (1,)), ((), ())), precision=lax.Precision.HIGHEST
    )
    lanes = lax.broadcasted_iota(jnp.int32, (1, 128), 1)
    rows16 = lax.broadcasted_iota(jnp.int32, (16, 128), 0)
    ones_row = jnp.where(lax.broadcasted_iota(jnp.int32, (32, CANDS_HERE), 0) == 0, 1.0, 0.0)
    out = []
    for e in range(ENVS_HERE):
        r = returns[0:1, e * CANDS_HERE : (e + 1) * CANDS_HERE]
        ret_ref[e : e + 1, :] = r
        lowest = jnp.min(r, axis=1, keepdims=True)
        highest = jnp.max(r, axis=1, keepdims=True)
        c = chosen[number, e : e + 1, :]
        w = c * (r - lowest + 1.0)
        hi, w1 = split(w)
        mid, w2 = split(w1)
        left = jnp.where(
            rows16 == 0,
            hi.astype(F32),
            jnp.where(rows16 == 1, mid.astype(F32), jnp.where(rows16 == 2, w2, jnp.where(rows16 == 3, c, 0.0))),
        ).astype(BF16)
        n = jnp.concatenate([noise[:, e * CANDS_HERE : (e + 1) * CANDS_HERE], ones_row], 0)
        n2_hi, n2_lo = split(n * n)
        right = jnp.concatenate([n.astype(BF16), n2_hi, n2_lo.astype(BF16)], 0)
        sums = lax.dot_general(left, right, (((1,), (1,)), ((), ())), preferred_element_type=F32)
        first_m, second_m = sums[:, :128], sums[:, 128:256] + sums[:, 256:]
        c1 = jnp.where(lanes == ONE + 1, highest, jnp.where(lanes == ONE + 2, lowest, first_m[3:4]))
        out += [
            first_m[0:1] + first_m[1:2] + first_m[2:3],
            c1,
            second_m[0:1] + second_m[1:2] + second_m[2:3],
            second_m[3:4],
        ]
    msg = jnp.concatenate(out, 0)
    for k in range(PEERS):
        msg_ref[k] = msg


def last_kernel(
    state_ref, got_ref, r0, r1, r2, b0, b1, mean_ref, spread_ref, ret_ref, best_ref
):
    state, best = refit(state_ref[...], got_ref[...])
    columns = jnp.transpose(state)
    lane = lax.broadcasted_iota(jnp.int32, (8, 128), 1)
    for e in range(ENVS_HERE):
        for ref, k in ((mean_ref, 2 * e), (spread_ref, 2 * e + 1)):
            table = jnp.zeros((8, 128), F32)
            for t in range(HOR):
                table = jnp.where(lane == t, columns[8 * t : 8 * t + 8, k : k + 1], table)
            for a in range(ACT):
                ref[a, e : e + 1, :] = table[a : a + 1, :HOR]
    for i, r in enumerate((r0, r1, r2)):
        ret_ref[i] = r[...]
    lane = lax.broadcasted_iota(jnp.int32, (ENVS_HERE, 128), 1)
    table = jnp.where(lane == 0, b0[...], jnp.where(lane == 1, b1[...], best))
    best_ref[...] = table[:, :ITERS]


VMEM = pl.BlockSpec(memory_space=pltpu.VMEM)


def rollout(number, weights, h0, z0, a_noise, s_noise, chosen, state, got):
    first = state is None
    shapes = [
        jax.ShapeDtypeStruct((ENVS_HERE, CANDS_HERE), F32),
        jax.ShapeDtypeStruct((PEERS, 8, 128), F32),
    ]
    args = [*weights, h0, z0, a_noise, s_noise, chosen]
    if not first:
        shapes += [
            jax.ShapeDtypeStruct((8, 128), F32),
            jax.ShapeDtypeStruct((ENVS_HERE, 128), F32),
        ]
        args += [state, got]
    return pl.pallas_call(
        functools.partial(rollout_kernel, first, number),
        out_shape=shapes,
        in_specs=[VMEM] * len(args),
        out_specs=[VMEM] * len(shapes),
        scratch_shapes=[pltpu.VMEM((ROWS, COLS), F32)],
        compiler_params=pltpu.CompilerParams(vmem_limit_bytes=40 << 20),
        name=f"rollout_{number}",
    )(*args)


PART = 1355
ROW = 200
TABLE = 1736


def prepare_kernel(own, other, w_h, w_x, w_1, w_5, w_6z, w_r, w_7, blocks, left, right, fifth_l, fifth_r):
    here = lax.axis_index("cand")
    y, core = here // 2, here % 2
    for k in range(4):
        there = (y // 2 ^ k // 2) * 2 + (y % 2 ^ k % 2)
        blocks[there * 2 + core] = own[k]
        blocks[there * 2 + 1 - core] = other[k]

    row = lax.broadcasted_iota(jnp.int32, (8, 128), 0)
    lane = lax.broadcasted_iota(jnp.int32, (8, 128), 1)
    for env in range(32):
        for cand in range(PEERS):
            start, first_lane = divmod(PART * (env * PEERS + cand), ROW)
            block = blocks[cand, env].astype(F32)
            for half, table in ((0, left), (1, right)):
                piece = block[:, 128 * half : 128 * half + 128]
                at = table.at[start : start + 8, :]
                if first_lane > 128 * half:
                    mask = (row > 0) | (lane >= first_lane - 128 * half)
                    pltpu.store(at, piece, mask=mask)
                else:
                    at[...] = piece

    def rows(start, count, step=1):
        at = pl.ds(start, count, stride=step) if step > 1 else pl.ds(start, count)
        return jnp.concatenate([left[at, :], right[at, :]], 1)

    row8 = lax.broadcasted_iota(jnp.int32, (8, 256), 0)
    lane8 = lax.broadcasted_iota(jnp.int32, (8, 256), 1)

    def foot(bias, fan_in, ones=0.0):
        bias = jnp.broadcast_to(bias * (bias_scale * fan_in**0.5), (8, 256))
        if ones:
            bias = jnp.where((lane8 == 200) | (lane8 == 201), ones, bias)
        hi = bias.astype(BF16).astype(F32)
        return jnp.where(row8 == 0, hi, jnp.where(row8 == 1, bias - hi, 0.0))

    def filled(parts, count=256):
        used = sum(part.shape[0] for part in parts)
        if used < count:
            parts = [*parts, jnp.zeros((count - used, 256), F32)]
        return jnp.concatenate(parts, 0).astype(BF16)

    first = rows(0, 37)
    state_rows = jnp.where(lax.broadcasted_iota(jnp.int32, (32, 256), 0) < STOCH, first[:32], 0.0)
    action_rows = jnp.where(row8 < ACT, rows(STOCH, 8), 0.0)
    w_1[...] = filled([state_rows, action_rows, foot(rows(36, 1), 36, 6.0)], 128)
    w_x[:, :256] = filled([rows(37, 200, 2), foot(rows(837, 1), 400)])
    w_x[:, 256:512] = filled([rows(38, 200, 2), foot(rows(838, 1), 400, 2000.0)])
    w_h[:, :256] = filled([rows(437, 200, 2)])
    w_h[:, 256:512] = filled([rows(438, 200, 2)])
    w_x[:, 512:] = filled([rows(839, 200), foot(rows(1239, 1), 400)])
    w_r[...] = filled([rows(1039, 200)])
    w_h[:, 512:768] = filled([rows(1240, 200), foot(rows(1440, 1), 200, 200**0.5)])

    def fifth(k, count):
        down, at = divmod(60 * k, ROW)
        piece = pltpu.roll(rows(1441 + down, count, 3), (256 - at) % 256, 1) if at else rows(1441 + down, count, 3)
        if at + 60 > ROW:
            more = pltpu.roll(rows(1442 + down, count, 3), ROW - at, 1)
            lanes = lax.broadcasted_iota(jnp.int32, (count, 256), 1)
            piece = jnp.where(lanes < ROW - at, piece, more)
        return piece

    def halves(piece):
        piece = piece[:, :128]
        lanes = lax.broadcasted_iota(jnp.int32, piece.shape, 1)
        return (
            jnp.where(lanes < STOCH, piece, 0.0),
            jnp.where(lanes < STOCH, pltpu.roll(piece, 128 - STOCH, 1), 0.0),
        )

    for k in range(10):
        mean, scale = halves(fifth(k, 20))
        fifth_l[pl.ds(k, 20, stride=10), :] = mean
        fifth_r[pl.ds(k, 20, stride=10), :] = scale
    last_row = rows(1501, 8)
    mean, scale = halves(last_row)
    bias = jnp.concatenate([mean, scale], 1)[0:1]
    w_5[...] = filled([jnp.concatenate([fifth_l[...], fifth_r[...]], 1), foot(bias, 200)])

    def shifted(start, count):
        one = pltpu.roll(rows(start, count), 256 - 60, 1)
        two = pltpu.roll(rows(start + 1, count), ROW - 60, 1)
        lanes = lax.broadcasted_iota(jnp.int32, (count, 256), 1)
        return jnp.where(lanes < ROW - 60, one, jnp.where(lanes < ROW, two, 0.0))

    w_h[:, 768:] = filled([shifted(1501, 200), foot(shifted(1731, 1), 230, 230**0.5)])
    below = shifted(1701, 32)
    below = jnp.where(lax.broadcasted_iota(jnp.int32, (32, 256), 0) < STOCH, below, 0.0)
    w_6z[...] = filled([below], 128)
    weight = shifted(1732, 1) * S200
    last_bias = pltpu.roll(rows(1733, 1), ROW - 60, 1) * bias_scale
    lanes = lax.broadcasted_iota(jnp.int32, (1, 256), 1)
    weight = jnp.where(lanes < ROW, weight, jnp.where(lanes == ROW, last_bias, 0.0))
    w_7[...] = jnp.broadcast_to(weight, (8, 256))


def prepared(own, other):
    return pl.pallas_call(
        prepare_kernel,
        out_shape=[
            jax.ShapeDtypeStruct((256, 1024), BF16),
            jax.ShapeDtypeStruct((256, 768), BF16),
            jax.ShapeDtypeStruct((128, 256), BF16),
            jax.ShapeDtypeStruct((256, 256), BF16),
            jax.ShapeDtypeStruct((128, 256), BF16),
            jax.ShapeDtypeStruct((256, 256), BF16),
            jax.ShapeDtypeStruct((8, 256), F32),
        ],
        in_specs=[VMEM] * 2,
        out_specs=[VMEM] * 7,
        scratch_shapes=[
            pltpu.VMEM((PEERS, 32, 8, 256), BF16),
            pltpu.VMEM((TABLE, 128), F32),
            pltpu.VMEM((TABLE, 128), F32),
            pltpu.VMEM((200, 128), F32),
            pltpu.VMEM((200, 128), F32),
        ],
        compiler_params=pltpu.CompilerParams(vmem_limit_bytes=40 << 20),
        name="prepare",
    )(own, other)


def gathered_params(shard):
    start = (lax.axis_index("env") * PEERS + lax.axis_index("cand")) * PART % ROW
    block = lax.dynamic_update_slice(jnp.zeros(8 * ROW, BF16), shard, (start,)).reshape(8, ROW)
    block = jnp.pad(block, ((0, 0), (0, 256 - ROW)))
    block = lax.all_to_all(jnp.broadcast_to(block[None], (32, 8, 256)), "env", 0, 0, tiled=True)
    near = [lax.ppermute(block, "cand", [(i, i ^ 2 * k) for i in range(PEERS)]) for k in (1, 2, 3)]
    own = jnp.stack([block, *near])
    return own, lax.ppermute(own, "cand", [(i, i ^ 1) for i in range(PEERS)])


def body(params, h_start, z_start, action_noise, state_noise, elites):
    a_noise = jnp.pad(
        action_noise.reshape(ITERS, HOR, ACT, COLS), ((0, 0), (0, 0), (0, 8 - ACT), (0, 0))
    ).reshape(ITERS, ROWS, COLS)
    s_noise = jnp.pad(
        state_noise.reshape(ITERS, HOR, STOCH, COLS), ((0, 0), (0, 0), (0, 32 - STOCH), (0, 0))
    )

    h0 = jnp.concatenate(
        [h_start, jnp.ones((ENVS_HERE, 2), F32), jnp.zeros((ENVS_HERE, 54), F32)], 1
    )
    z0 = jnp.pad(z_start, ((0, 0), (0, 128 - STOCH)))
    ids = lax.axis_index("cand") * CANDS_HERE + jnp.arange(CANDS_HERE, dtype=jnp.int32)
    chosen = jnp.any(elites[:, :, :, None] == ids, axis=2).astype(F32)

    weights = prepared(*gathered_params(params))
    rets, bests = [], []
    state = got = None
    for number in range(ITERS):
        out = rollout(number, weights, h0, z0, a_noise, s_noise, chosen, state, got)
        rets.append(out[0])
        if number == 0:
            state = jnp.broadcast_to(
                jnp.array([0.0, 1.0, 0.0, 1.0, 0.0, 0.0, 0.0, 0.0], F32)[:, None], (8, 128)
            )
        else:
            state = out[2]
            bests.append(out[3])
        got = lax.all_to_all(out[1], "cand", 0, 0, tiled=True)
    mean, spread, returns, best = pl.pallas_call(
        last_kernel,
        out_shape=[
            jax.ShapeDtypeStruct((ACT, ENVS_HERE, HOR), F32),
            jax.ShapeDtypeStruct((ACT, ENVS_HERE, HOR), F32),
            jax.ShapeDtypeStruct((ITERS, ENVS_HERE, CANDS_HERE), F32),
            jax.ShapeDtypeStruct((ENVS_HERE, ITERS), F32),
        ],
        in_specs=[VMEM] * 7,
        out_specs=[VMEM] * 4,
        name="last",
    )(state, got, *rets, *bests)
    return mean.transpose(2, 0, 1), spread.transpose(2, 0, 1), returns, best.T


def solution(mesh):
    placed = (
        P(("env", "cand")),
        P("env", None),
        P("env", None),
        P(None, None, None, "env", "cand"),
        P(None, None, None, "env", "cand"),
        P(None, "env", None),
    )
    return jax.shard_map(
        body,
        mesh=mesh,
        in_specs=placed,
        out_specs=(
            P(None, None, "env"),
            P(None, None, "env"),
            P(None, "env", "cand"),
            P(None, "env"),
        ),
        check_vma=False,
    )
```

```python
import functools

import jax
import jax.numpy as jnp
from jax import lax
from jax.experimental import pallas as pl
from jax.experimental.pallas import tpu as pltpu
from jax.sharding import PartitionSpec as P

D_DET = 200
STOCH = 30
HID = 200
ACT = 6
HOR = 12
ITERS = 3

PEERS = 8
ENVS_HERE = 2
CANDS_HERE = 128
COLS = ENVS_HERE * CANDS_HERE

WIDE = 208
DEEP = 256
ROWS = 96
ONE = 96

bias_scale = 0.2
min_scale = 0.1
variance_floor = 1e-05

S36, S400, S200, S230 = (float(n) ** -0.5 for n in (36, 400, 200, 230))
LOG2E = 1.4426950408889634

F32, BF16 = jnp.float32, jnp.bfloat16


def dot(a, b):
    return jnp.dot(a, b, preferred_element_type=F32)


def dot_t(a, b):
    return lax.dot_general(a, b, (((1,), (1,)), ((), ())), preferred_element_type=F32)


def scaled_elu(y, scale):
    return jnp.where(y > 0, y * scale, jnp.exp2(y * (scale * LOG2E)) - 1.0)


def softplus(v):
    return jnp.maximum(v, 0.0) + jnp.log(1.0 + jnp.exp(-jnp.abs(v)))


def refit(state, gathered):
    rows = []
    best = []
    for e in range(ENVS_HERE):
        m1, c1, m2, c2 = (gathered[:, 4 * e + k, :] for k in range(4))
        lowest = c1[:, ONE + 2 : ONE + 3]
        highest = c1[:, ONE + 1 : ONE + 2]
        worst = jnp.min(lowest, axis=0, keepdims=True)
        best.append(jnp.max(highest, axis=0, keepdims=True))
        lift = lowest - worst
        m1 = jnp.sum(m1 + lift * c1, axis=0, keepdims=True)
        m2 = jnp.sum(m2 + lift * c2, axis=0, keepdims=True)
        total = m1[:, ONE : ONE + 1]
        m1 = m1 / total
        m2 = m2 / total
        center = state[2 * e : 2 * e + 1]
        spread = state[2 * e + 1 : 2 * e + 2]
        rows.append(center + spread * m1)
        rows.append(
            jnp.sqrt(spread * spread * jnp.maximum(m2 - m1 * m1, 0.0) + variance_floor)
        )
    state = jnp.concatenate(rows + [jnp.zeros((4, 128), F32)], 0)
    return state, jnp.concatenate([jnp.broadcast_to(b, (1, 128)) for b in best], 0)


def split(v):
    hi = v.astype(BF16)
    return hi, v - hi.astype(F32)


def rollout_kernel(
    first, number, w_h, w_x, w_1, w_5, w_6z, w_r, w_7, h0, z0, a_noise, s_noise, chosen, *rest
):
    if first:
        ret_ref, msg_ref, acts = rest
    else:
        state_ref, got_ref, ret_ref, msg_ref, new_state_ref, best_ref, acts = rest
    noise = a_noise[number].astype(F32)
    if first:
        acts[...] = noise
    else:
        state, best = refit(state_ref[...], got_ref[...])
        new_state_ref[...] = state
        best_ref[...] = best
        columns = jnp.transpose(state)
        for e in range(ENVS_HERE):
            at = pl.ds(e * CANDS_HERE, CANDS_HERE)
            center = columns[:ROWS, 2 * e : 2 * e + 1]
            spread = columns[:ROWS, 2 * e + 1 : 2 * e + 2]
            acts[:, at] = center + spread * noise[:, e * CANDS_HERE : (e + 1) * CANDS_HERE]
    ones8 = jnp.where(lax.broadcasted_iota(jnp.int32, (8, COLS), 0) < 2, 1.0, 0.0).astype(F32)
    filler = jnp.zeros((80, COLS), F32)
    in_latent = lax.broadcasted_iota(jnp.int32, (1, 128), 1) < 32

    def drawn(t, n):
        block = jnp.concatenate([n, acts[t * 8 : t * 8 + 8, :], ones8, filler], 0)
        return jnp.transpose(block)

    def spread_out(ref):
        return jnp.concatenate(
            [jnp.broadcast_to(ref[e : e + 1, :], (CANDS_HERE, ref.shape[1])) for e in range(ENVS_HERE)], 0
        )

    h = spread_out(h0)
    q_sum = None
    for t in range(HOR + 1):
        hd = h.astype(BF16)
        if t == 0:
            za = (spread_out(z0) + drawn(0, jnp.zeros((32, COLS), F32))).astype(BF16)
        else:
            p = scaled_elu(dot(hd, w_h[:, 512:768]), S200).astype(BF16)
            s = dot(p, w_5[...]) * S200
            scale = jnp.where(in_latent, softplus(s[:, 128:]) + min_scale, 1.0)
            n = s_noise[number, t - 1].astype(F32)
            za = (s[:, :128] + scale * drawn(min(t, HOR - 1), n)).astype(BF16)
            q = scaled_elu(dot(hd, w_h[:, 768:]) + dot(za, w_6z[...]), S230)
            q = q.astype(BF16).astype(F32)
            q_sum = q if q_sum is None else q_sum + q
        if t == HOR:
            break
        x = scaled_elu(dot(za, w_1[...]), S36).astype(BF16)
        gates = dot(x, w_x[:, :512]) + dot(hd, w_h[:, :512])
        half = 0.5 * h
        rh = (half + jnp.tanh(gates[:, :256] * (0.5 * S400)) * half).astype(BF16)
        update = 0.5 + 0.5 * jnp.tanh(gates[:, 256:] * (0.5 * S400))
        proposal = jnp.tanh((dot(x, w_x[:, 512:]) + dot(rh, w_r[...])) * S400)
        h = proposal + update * (h - proposal)

    wide = lax.broadcasted_iota(jnp.int32, (1, COLS), 1)
    wide16 = lax.broadcasted_iota(jnp.int32, (16, COLS), 1) // CANDS_HERE
    rows16 = lax.broadcasted_iota(jnp.int32, (16, COLS), 0)
    lanes = lax.broadcasted_iota(jnp.int32, (1, 128), 1)

    weight = jnp.where(rows16 == 0, w_7[0:1, :], 0.0).astype(BF16)
    part_1, left_over = split(q_sum)
    part_2, left_over = split(left_over)
    r = dot_t(weight, part_1) + (dot_t(weight, part_2) + dot_t(weight, left_over.astype(BF16)))
    n = jnp.concatenate(
        [noise, jnp.where(lax.broadcasted_iota(jnp.int32, (32, COLS), 0) == 0, 1.0, 0.0)], 0
    )
    n2_hi, n2_lo = split(n * n)
    r = r[0:1] * S200 + w_7[1:2, :]
    ends = []
    for e in range(ENVS_HERE):
        mine = r[:, e * CANDS_HERE : (e + 1) * CANDS_HERE]
        ret_ref[e : e + 1, :] = mine
        ends.append((jnp.min(mine, axis=1, keepdims=True), jnp.max(mine, axis=1, keepdims=True)))
    lowest = jnp.where(wide < CANDS_HERE, ends[0][0], ends[1][0])
    c = jnp.concatenate([chosen[number, e : e + 1, :] for e in range(ENVS_HERE)], 1)
    w = c * (r - lowest + 1.0)
    hi, w1 = split(w)
    mid, w2 = split(w1)
    kind = rows16 % 4
    left = jnp.where(
        kind == 0, hi.astype(F32), jnp.where(kind == 1, mid.astype(F32), jnp.where(kind == 2, w2, c))
    )
    left = jnp.where(rows16 // 4 == wide16, left, 0.0).astype(BF16)
    sums = dot_t(left, jnp.concatenate([n.astype(BF16), n2_hi, n2_lo.astype(BF16)], 0))
    first_m, second_m = sums[:8, :128], sums[:8, 128:256] + sums[:8, 256:]
    out = []
    for e in range(ENVS_HERE):
        k = 4 * e
        lowest, highest = ends[e]
        out += [
            first_m[k : k + 1] + first_m[k + 1 : k + 2] + first_m[k + 2 : k + 3],
            jnp.where(
                lanes == ONE + 1, highest, jnp.where(lanes == ONE + 2, lowest, first_m[k + 3 : k + 4])
            ),
            second_m[k : k + 1] + second_m[k + 1 : k + 2] + second_m[k + 2 : k + 3],
            second_m[k + 3 : k + 4],
        ]
    msg = jnp.concatenate(out, 0)
    for k in range(PEERS):
        msg_ref[k] = msg


def last_kernel(
    state_ref, got_ref, r0, r1, r2, b0, b1, mean_ref, spread_ref, ret_ref, best_ref
):
    state, best = refit(state_ref[...], got_ref[...])
    columns = jnp.transpose(state)
    lane = lax.broadcasted_iota(jnp.int32, (8, 128), 1)
    for e in range(ENVS_HERE):
        for ref, k in ((mean_ref, 2 * e), (spread_ref, 2 * e + 1)):
            table = jnp.zeros((8, 128), F32)
            for t in range(HOR):
                table = jnp.where(lane == t, columns[8 * t : 8 * t + 8, k : k + 1], table)
            for a in range(ACT):
                ref[a, e : e + 1, :] = table[a : a + 1, :HOR]
    for i, r in enumerate((r0, r1, r2)):
        ret_ref[i] = r[...]
    lane = lax.broadcasted_iota(jnp.int32, (ENVS_HERE, 128), 1)
    table = jnp.where(lane == 0, b0[...], jnp.where(lane == 1, b1[...], best))
    best_ref[...] = table[:, :ITERS]


VMEM = pl.BlockSpec(memory_space=pltpu.VMEM)


def rollout(number, weights, h0, z0, a_noise, s_noise, chosen, state, got):
    first = state is None
    shapes = [
        jax.ShapeDtypeStruct((ENVS_HERE, CANDS_HERE), F32),
        jax.ShapeDtypeStruct((PEERS, 8, 128), F32),
    ]
    args = [*weights, h0, z0, a_noise, s_noise, chosen]
    if not first:
        shapes += [
            jax.ShapeDtypeStruct((8, 128), F32),
            jax.ShapeDtypeStruct((ENVS_HERE, 128), F32),
        ]
        args += [state, got]
    return pl.pallas_call(
        functools.partial(rollout_kernel, first, number),
        out_shape=shapes,
        in_specs=[VMEM] * len(args),
        out_specs=[VMEM] * len(shapes),
        scratch_shapes=[pltpu.VMEM((ROWS, COLS), F32)],
        compiler_params=pltpu.CompilerParams(vmem_limit_bytes=40 << 20),
        name=f"rollout_{number}",
    )(*args)


PART = 1355
ROW = 200
TABLE = 1736


def prepare_kernel(own, other, w_h, w_x, w_1, w_5, w_6z, w_r, w_7, blocks, left, right, fifth_l, fifth_r):
    here = lax.axis_index("cand")
    y, core = here // 2, here % 2
    for k in range(4):
        there = (y // 2 ^ k // 2) * 2 + (y % 2 ^ k % 2)
        blocks[there * 2 + core] = own[k]
        blocks[there * 2 + 1 - core] = other[k]

    row = lax.broadcasted_iota(jnp.int32, (8, 128), 0)
    lane = lax.broadcasted_iota(jnp.int32, (8, 128), 1)
    for env in range(32):
        for cand in range(PEERS):
            start, first_lane = divmod(PART * (env * PEERS + cand), ROW)
            block = blocks[cand, env].astype(F32)
            for half, table in ((0, left), (1, right)):
                piece = block[:, 128 * half : 128 * half + 128]
                at = table.at[start : start + 8, :]
                if first_lane > 128 * half:
                    mask = (row > 0) | (lane >= first_lane - 128 * half)
                    pltpu.store(at, piece, mask=mask)
                else:
                    at[...] = piece

    def rows(start, count, step=1):
        at = pl.ds(start, count, stride=step) if step > 1 else pl.ds(start, count)
        return jnp.concatenate([left[at, :], right[at, :]], 1)

    row8 = lax.broadcasted_iota(jnp.int32, (8, 256), 0)
    lane8 = lax.broadcasted_iota(jnp.int32, (8, 256), 1)

    def foot(bias, fan_in, ones=0.0):
        bias = jnp.broadcast_to(bias * (bias_scale * fan_in**0.5), (8, 256))
        if ones:
            bias = jnp.where((lane8 == 200) | (lane8 == 201), ones, bias)
        hi = bias.astype(BF16).astype(F32)
        return jnp.where(row8 == 0, hi, jnp.where(row8 == 1, bias - hi, 0.0))

    def filled(parts, count=256):
        used = sum(part.shape[0] for part in parts)
        if used < count:
            parts = [*parts, jnp.zeros((count - used, 256), F32)]
        return jnp.concatenate(parts, 0).astype(BF16)

    first = rows(0, 37)
    state_rows = jnp.where(lax.broadcasted_iota(jnp.int32, (32, 256), 0) < STOCH, first[:32], 0.0)
    action_rows = jnp.where(row8 < ACT, rows(STOCH, 8), 0.0)
    w_1[...] = filled([state_rows, action_rows, foot(rows(36, 1), 36, 6.0)], 128)
    w_x[:, :256] = filled([rows(37, 200, 2), foot(rows(837, 1), 400)])
    w_x[:, 256:512] = filled([rows(38, 200, 2), foot(rows(838, 1), 400, 2000.0)])
    w_h[:, :256] = filled([rows(437, 200, 2)])
    w_h[:, 256:512] = filled([rows(438, 200, 2)])
    w_x[:, 512:] = filled([rows(839, 200), foot(rows(1239, 1), 400)])
    w_r[...] = filled([rows(1039, 200)])
    w_h[:, 512:768] = filled([rows(1240, 200), foot(rows(1440, 1), 200, 200**0.5)])

    def fifth(k, count):
        down, at = divmod(60 * k, ROW)
        piece = pltpu.roll(rows(1441 + down, count, 3), (256 - at) % 256, 1) if at else rows(1441 + down, count, 3)
        if at + 60 > ROW:
            more = pltpu.roll(rows(1442 + down, count, 3), ROW - at, 1)
            lanes = lax.broadcasted_iota(jnp.int32, (count, 256), 1)
            piece = jnp.where(lanes < ROW - at, piece, more)
        return piece

    def halves(piece):
        piece = piece[:, :128]
        lanes = lax.broadcasted_iota(jnp.int32, piece.shape, 1)
        return (
            jnp.where(lanes < STOCH, piece, 0.0),
            jnp.where(lanes < STOCH, pltpu.roll(piece, 128 - STOCH, 1), 0.0),
        )

    for k in range(10):
        mean, scale = halves(fifth(k, 20))
        fifth_l[pl.ds(k, 20, stride=10), :] = mean
        fifth_r[pl.ds(k, 20, stride=10), :] = scale
    last_row = rows(1501, 8)
    mean, scale = halves(last_row)
    bias = jnp.concatenate([mean, scale], 1)[0:1]
    w_5[...] = filled([jnp.concatenate([fifth_l[...], fifth_r[...]], 1), foot(bias, 200)])

    def shifted(start, count):
        one = pltpu.roll(rows(start, count), 256 - 60, 1)
        two = pltpu.roll(rows(start + 1, count), ROW - 60, 1)
        lanes = lax.broadcasted_iota(jnp.int32, (count, 256), 1)
        return jnp.where(lanes < ROW - 60, one, jnp.where(lanes < ROW, two, 0.0))

    w_h[:, 768:] = filled([shifted(1501, 200), foot(shifted(1731, 1), 230, 230**0.5)])
    below = shifted(1701, 32)
    below = jnp.where(lax.broadcasted_iota(jnp.int32, (32, 256), 0) < STOCH, below, 0.0)
    w_6z[...] = filled([below], 128)
    last_bias = left[1733:1734, 60:61] * (HOR * bias_scale)
    w_7[...] = jnp.where(row8 == 0, shifted(1732, 1), last_bias)


def prepared(own, other):
    return pl.pallas_call(
        prepare_kernel,
        out_shape=[
            jax.ShapeDtypeStruct((256, 1024), BF16),
            jax.ShapeDtypeStruct((256, 768), BF16),
            jax.ShapeDtypeStruct((128, 256), BF16),
            jax.ShapeDtypeStruct((256, 256), BF16),
            jax.ShapeDtypeStruct((128, 256), BF16),
            jax.ShapeDtypeStruct((256, 256), BF16),
            jax.ShapeDtypeStruct((8, 256), F32),
        ],
        in_specs=[VMEM] * 2,
        out_specs=[VMEM] * 7,
        scratch_shapes=[
            pltpu.VMEM((PEERS, 32, 8, 256), BF16),
            pltpu.VMEM((TABLE, 128), F32),
            pltpu.VMEM((TABLE, 128), F32),
            pltpu.VMEM((200, 128), F32),
            pltpu.VMEM((200, 128), F32),
        ],
        compiler_params=pltpu.CompilerParams(vmem_limit_bytes=40 << 20),
        name="prepare",
    )(own, other)


def from_env(shard):
    start = (lax.axis_index("env") * PEERS + lax.axis_index("cand")) * PART % ROW
    block = lax.dynamic_update_slice(jnp.zeros(8 * ROW, BF16), shard, (start,)).reshape(8, ROW)
    block = jnp.pad(block, ((0, 0), (0, 256 - ROW)))
    return lax.all_to_all(jnp.broadcast_to(block[None], (32, 8, 256)), "env", 0, 0, tiled=True)


def body(params, h_start, z_start, action_noise, state_noise, elites):
    block = from_env(params)
    block, h_start, z_start, action_noise, state_noise, elites = lax.optimization_barrier(
        (block, h_start, z_start, action_noise, state_noise, elites)
    )
    near = [lax.ppermute(block, "cand", [(i, i ^ 2 * k) for i in range(PEERS)]) for k in (1, 2, 3)]
    a_noise = jnp.pad(
        action_noise.reshape(ITERS, HOR, ACT, COLS), ((0, 0), (0, 0), (0, 8 - ACT), (0, 0))
    ).reshape(ITERS, ROWS, COLS)
    s_noise = jnp.pad(
        state_noise.reshape(ITERS, HOR, STOCH, COLS), ((0, 0), (0, 0), (0, 32 - STOCH), (0, 0))
    )

    h0 = jnp.concatenate(
        [h_start, jnp.ones((ENVS_HERE, 2), F32), jnp.zeros((ENVS_HERE, 54), F32)], 1
    )
    z0 = jnp.pad(z_start, ((0, 0), (0, 128 - STOCH)))
    ids = lax.axis_index("cand") * CANDS_HERE + jnp.arange(CANDS_HERE, dtype=jnp.int32)
    chosen = jnp.any(elites[:, :, :, None] == ids, axis=2).astype(F32)

    near, a_noise, s_noise, h0, z0, chosen = lax.optimization_barrier(
        (near, a_noise, s_noise, h0, z0, chosen)
    )
    own = jnp.stack([block, *near])
    other = lax.ppermute(own, "cand", [(i, i ^ 1) for i in range(PEERS)])
    weights = prepared(own, other)
    rets, bests = [], []
    state = got = None
    for number in range(ITERS):
        out = rollout(number, weights, h0, z0, a_noise, s_noise, chosen, state, got)
        rets.append(out[0])
        if number == 0:
            state = jnp.broadcast_to(
                jnp.array([0.0, 1.0, 0.0, 1.0, 0.0, 0.0, 0.0, 0.0], F32)[:, None], (8, 128)
            )
        else:
            state = out[2]
            bests.append(out[3])
        got = lax.all_to_all(out[1], "cand", 0, 0, tiled=True)
    mean, spread, returns, best = pl.pallas_call(
        last_kernel,
        out_shape=[
            jax.ShapeDtypeStruct((ACT, ENVS_HERE, HOR), F32),
            jax.ShapeDtypeStruct((ACT, ENVS_HERE, HOR), F32),
            jax.ShapeDtypeStruct((ITERS, ENVS_HERE, CANDS_HERE), F32),
            jax.ShapeDtypeStruct((ENVS_HERE, ITERS), F32),
        ],
        in_specs=[VMEM] * 7,
        out_specs=[VMEM] * 4,
        compiler_params=pltpu.CompilerParams(vmem_limit_bytes=4 << 20),
        name="last",
    )(state, got, *rets, *bests)
    return mean.transpose(2, 0, 1), spread.transpose(2, 0, 1), returns, best.T


def solution(mesh):
    placed = (
        P(("env", "cand")),
        P("env", None),
        P("env", None),
        P(None, None, None, "env", "cand"),
        P(None, None, None, "env", "cand"),
        P(None, "env", None),
    )
    return jax.shard_map(
        body,
        mesh=mesh,
        in_specs=placed,
        out_specs=(
            P(None, None, "env"),
            P(None, None, "env"),
            P(None, "env", "cand"),
            P(None, "env"),
        ),
        check_vma=False,
    )
```

```python
import functools

import jax
import jax.numpy as jnp
from jax import lax
from jax.experimental import pallas as pl
from jax.experimental.pallas import tpu as pltpu
from jax.sharding import PartitionSpec as P

D_DET = 200
STOCH = 30
HID = 200
ACT = 6
HOR = 12
ITERS = 3

PEERS = 8
ENVS_HERE = 2
CANDS_HERE = 128
COLS = ENVS_HERE * CANDS_HERE

WIDE = 208
DEEP = 256
ROWS = 96
ONE = 96

bias_scale = 0.2
min_scale = 0.1
variance_floor = 1e-05

S36, S400, S200, S230 = (float(n) ** -0.5 for n in (36, 400, 200, 230))
LOG2E = 1.4426950408889634

F32, BF16 = jnp.float32, jnp.bfloat16


def dot(a, b):
    return jnp.dot(a, b, preferred_element_type=F32)


def dot_t(a, b):
    return lax.dot_general(a, b, (((1,), (1,)), ((), ())), preferred_element_type=F32)


def scaled_elu(y, scale):
    return jnp.where(y > 0, y * scale, jnp.exp2(y * (scale * LOG2E)) - 1.0)


def softplus(v):
    return jnp.maximum(v, 0.0) + jnp.log(1.0 + jnp.exp(-jnp.abs(v)))


def refit(state, gathered):
    rows = []
    best = []
    for e in range(ENVS_HERE):
        m1, c1, m2, c2 = (gathered[:, 4 * e + k, :] for k in range(4))
        lowest = c1[:, ONE + 2 : ONE + 3]
        highest = c1[:, ONE + 1 : ONE + 2]
        worst = jnp.min(lowest, axis=0, keepdims=True)
        best.append(jnp.max(highest, axis=0, keepdims=True))
        lift = lowest - worst
        m1 = jnp.sum(m1 + lift * c1, axis=0, keepdims=True)
        m2 = jnp.sum(m2 + lift * c2, axis=0, keepdims=True)
        total = m1[:, ONE : ONE + 1]
        m1 = m1 / total
        m2 = m2 / total
        center = state[2 * e : 2 * e + 1]
        spread = state[2 * e + 1 : 2 * e + 2]
        rows.append(center + spread * m1)
        rows.append(
            jnp.sqrt(spread * spread * jnp.maximum(m2 - m1 * m1, 0.0) + variance_floor)
        )
    state = jnp.concatenate(rows + [jnp.zeros((4, 128), F32)], 0)
    return state, jnp.concatenate([jnp.broadcast_to(b, (1, 128)) for b in best], 0)


def split(v):
    hi = v.astype(BF16)
    return hi, v - hi.astype(F32)


def rollout_kernel(
    first, number, w_h, w_x, w_1, w_5, w_6z, w_r, w_7, h0, z0, a_noise, s_noise, chosen, *rest
):
    if first:
        ret_ref, msg_ref, acts = rest
    else:
        state_ref, got_ref, ret_ref, msg_ref, new_state_ref, best_ref, acts = rest
    noise = a_noise[number].astype(F32)
    if first:
        acts[...] = noise
    else:
        state, best = refit(state_ref[...], got_ref[...])
        new_state_ref[...] = state
        best_ref[...] = best
        columns = jnp.transpose(state)
        for e in range(ENVS_HERE):
            at = pl.ds(e * CANDS_HERE, CANDS_HERE)
            center = columns[:ROWS, 2 * e : 2 * e + 1]
            spread = columns[:ROWS, 2 * e + 1 : 2 * e + 2]
            acts[:, at] = center + spread * noise[:, e * CANDS_HERE : (e + 1) * CANDS_HERE]
    ones8 = jnp.where(lax.broadcasted_iota(jnp.int32, (8, COLS), 0) < 2, 1.0, 0.0).astype(F32)
    filler = jnp.zeros((80, COLS), F32)
    in_latent = lax.broadcasted_iota(jnp.int32, (1, 128), 1) < 32

    def drawn(t, n):
        block = jnp.concatenate([n, acts[t * 8 : t * 8 + 8, :], ones8, filler], 0)
        return jnp.transpose(block)

    def spread_out(ref):
        return jnp.concatenate(
            [jnp.broadcast_to(ref[e : e + 1, :], (CANDS_HERE, ref.shape[1])) for e in range(ENVS_HERE)], 0
        )

    h = spread_out(h0)
    q_sum = None
    for t in range(HOR + 1):
        hd = h.astype(BF16)
        if t == 0:
            za = (spread_out(z0) + drawn(0, jnp.zeros((32, COLS), F32))).astype(BF16)
        else:
            p = scaled_elu(dot(hd, w_h[:, 512:768]), S200).astype(BF16)
            s = dot(p, w_5[...]) * S200
            scale = jnp.where(in_latent, softplus(s[:, 128:]) + min_scale, 1.0)
            n = s_noise[number, t - 1].astype(F32)
            za = (s[:, :128] + scale * drawn(min(t, HOR - 1), n)).astype(BF16)
        if t == HOR:
            q = scaled_elu(dot(hd, w_h[:, 768:]) + dot(za[:, :48], w_6z[:48]), S230)
            q = q.astype(BF16).astype(F32)
            q_sum = q if q_sum is None else q_sum + q
            break
        x = scaled_elu(dot(za[:, :48], w_1[:48]), S36).astype(BF16)
        gates = dot(x, w_x[:, :512]) + dot(hd, w_h[:, :512])
        half = 0.5 * h
        rh = (half + jnp.tanh(gates[:, :256] * (0.5 * S400)) * half).astype(BF16)
        update = 0.5 + 0.5 * jnp.tanh(gates[:, 256:] * (0.5 * S400))
        proposal = jnp.tanh((dot(x, w_x[:, 512:]) + dot(rh, w_r[...])) * S400)
        h = proposal + update * (h - proposal)
        if t > 0:
            q = scaled_elu(dot(hd, w_h[:, 768:]) + dot(za[:, :48], w_6z[:48]), S230)
            q = q.astype(BF16).astype(F32)
            q_sum = q if q_sum is None else q_sum + q

    wide = lax.broadcasted_iota(jnp.int32, (1, COLS), 1)
    wide16 = lax.broadcasted_iota(jnp.int32, (16, COLS), 1) // CANDS_HERE
    rows16 = lax.broadcasted_iota(jnp.int32, (16, COLS), 0)
    lanes = lax.broadcasted_iota(jnp.int32, (1, 128), 1)

    weight = jnp.where(rows16 == 0, w_7[0:1, :], 0.0).astype(BF16)
    part_1, left_over = split(q_sum)
    part_2, left_over = split(left_over)
    r = dot_t(weight, part_1) + (dot_t(weight, part_2) + dot_t(weight, left_over.astype(BF16)))
    n = jnp.concatenate(
        [noise, jnp.where(lax.broadcasted_iota(jnp.int32, (32, COLS), 0) == 0, 1.0, 0.0)], 0
    )
    n2_hi, n2_lo = split(n * n)
    r = r[0:1] * S200 + w_7[1:2, :]
    ends = []
    for e in range(ENVS_HERE):
        mine = r[:, e * CANDS_HERE : (e + 1) * CANDS_HERE]
        ret_ref[e : e + 1, :] = mine
        ends.append((jnp.min(mine, axis=1, keepdims=True), jnp.max(mine, axis=1, keepdims=True)))
    lowest = jnp.where(wide < CANDS_HERE, ends[0][0], ends[1][0])
    c = jnp.concatenate([chosen[number, e : e + 1, :] for e in range(ENVS_HERE)], 1)
    w = c * (r - lowest + 1.0)
    hi, w1 = split(w)
    mid, w2 = split(w1)
    kind = rows16 % 4
    left = jnp.where(
        kind == 0, hi.astype(F32), jnp.where(kind == 1, mid.astype(F32), jnp.where(kind == 2, w2, c))
    )
    left = jnp.where(rows16 // 4 == wide16, left, 0.0).astype(BF16)
    sums = dot_t(left, jnp.concatenate([n.astype(BF16), n2_hi, n2_lo.astype(BF16)], 0))
    first_m, second_m = sums[:8, :128], sums[:8, 128:256] + sums[:8, 256:]
    out = []
    for e in range(ENVS_HERE):
        k = 4 * e
        lowest, highest = ends[e]
        out += [
            first_m[k : k + 1] + first_m[k + 1 : k + 2] + first_m[k + 2 : k + 3],
            jnp.where(
                lanes == ONE + 1, highest, jnp.where(lanes == ONE + 2, lowest, first_m[k + 3 : k + 4])
            ),
            second_m[k : k + 1] + second_m[k + 1 : k + 2] + second_m[k + 2 : k + 3],
            second_m[k + 3 : k + 4],
        ]
    msg = jnp.concatenate(out, 0)
    for k in range(PEERS):
        msg_ref[k] = msg


def last_kernel(
    state_ref, got_ref, r0, r1, r2, b0, b1, mean_ref, spread_ref, ret_ref, best_ref
):
    state, best = refit(state_ref[...], got_ref[...])
    columns = jnp.transpose(state)
    lane = lax.broadcasted_iota(jnp.int32, (8, 128), 1)
    for e in range(ENVS_HERE):
        for ref, k in ((mean_ref, 2 * e), (spread_ref, 2 * e + 1)):
            table = jnp.zeros((8, 128), F32)
            for t in range(HOR):
                table = jnp.where(lane == t, columns[8 * t : 8 * t + 8, k : k + 1], table)
            for a in range(ACT):
                ref[a, e : e + 1, :] = table[a : a + 1, :HOR]
    for i, r in enumerate((r0, r1, r2)):
        ret_ref[i] = r[...]
    lane = lax.broadcasted_iota(jnp.int32, (ENVS_HERE, 128), 1)
    table = jnp.where(lane == 0, b0[...], jnp.where(lane == 1, b1[...], best))
    best_ref[...] = table[:, :ITERS]


VMEM = pl.BlockSpec(memory_space=pltpu.VMEM)


def rollout(number, weights, h0, z0, a_noise, s_noise, chosen, state, got):
    first = state is None
    shapes = [
        jax.ShapeDtypeStruct((ENVS_HERE, CANDS_HERE), F32),
        jax.ShapeDtypeStruct((PEERS, 8, 128), F32),
    ]
    args = [*weights, h0, z0, a_noise, s_noise, chosen]
    if not first:
        shapes += [
            jax.ShapeDtypeStruct((8, 128), F32),
            jax.ShapeDtypeStruct((ENVS_HERE, 128), F32),
        ]
        args += [state, got]
    return pl.pallas_call(
        functools.partial(rollout_kernel, first, number),
        out_shape=shapes,
        in_specs=[VMEM] * len(args),
        out_specs=[VMEM] * len(shapes),
        scratch_shapes=[pltpu.VMEM((ROWS, COLS), F32)],
        compiler_params=pltpu.CompilerParams(vmem_limit_bytes=40 << 20),
        name=f"rollout_{number}",
    )(*args)


PART = 1355
ROW = 200
TABLE = 1736


def prepare_kernel(own, other, w_h, w_x, w_1, w_5, w_6z, w_r, w_7, blocks, left, right, fifth_l, fifth_r):
    here = lax.axis_index("cand")
    y, core = here // 2, here % 2
    for k in range(4):
        there = (y // 2 ^ k // 2) * 2 + (y % 2 ^ k % 2)
        blocks[there * 2 + core] = own[k]
        blocks[there * 2 + 1 - core] = other[k]

    row = lax.broadcasted_iota(jnp.int32, (8, 128), 0)
    lane = lax.broadcasted_iota(jnp.int32, (8, 128), 1)
    for env in range(32):
        for cand in range(PEERS):
            start, first_lane = divmod(PART * (env * PEERS + cand), ROW)
            block = blocks[cand, env].astype(F32)
            for half, table in ((0, left), (1, right)):
                piece = block[:, 128 * half : 128 * half + 128]
                at = table.at[start : start + 8, :]
                if first_lane > 128 * half:
                    mask = (row > 0) | (lane >= first_lane - 128 * half)
                    pltpu.store(at, piece, mask=mask)
                else:
                    at[...] = piece

    def rows(start, count, step=1):
        at = pl.ds(start, count, stride=step) if step > 1 else pl.ds(start, count)
        return jnp.concatenate([left[at, :], right[at, :]], 1)

    row8 = lax.broadcasted_iota(jnp.int32, (8, 256), 0)
    lane8 = lax.broadcasted_iota(jnp.int32, (8, 256), 1)

    def foot(bias, fan_in, ones=0.0):
        bias = jnp.broadcast_to(bias * (bias_scale * fan_in**0.5), (8, 256))
        if ones:
            bias = jnp.where((lane8 == 200) | (lane8 == 201), ones, bias)
        hi = bias.astype(BF16).astype(F32)
        return jnp.where(row8 == 0, hi, jnp.where(row8 == 1, bias - hi, 0.0))

    def filled(parts, count=256):
        used = sum(part.shape[0] for part in parts)
        if used < count:
            parts = [*parts, jnp.zeros((count - used, 256), F32)]
        return jnp.concatenate(parts, 0).astype(BF16)

    first = rows(0, 37)
    state_rows = jnp.where(lax.broadcasted_iota(jnp.int32, (32, 256), 0) < STOCH, first[:32], 0.0)
    action_rows = jnp.where(row8 < ACT, rows(STOCH, 8), 0.0)
    w_1[...] = filled([state_rows, action_rows, foot(rows(36, 1), 36, 6.0)], 128)
    w_x[:, :256] = filled([rows(37, 200, 2), foot(rows(837, 1), 400)])
    w_x[:, 256:512] = filled([rows(38, 200, 2), foot(rows(838, 1), 400, 2000.0)])
    w_h[:, :256] = filled([rows(437, 200, 2)])
    w_h[:, 256:512] = filled([rows(438, 200, 2)])
    w_x[:, 512:] = filled([rows(839, 200), foot(rows(1239, 1), 400)])
    w_r[...] = filled([rows(1039, 200)])
    w_h[:, 512:768] = filled([rows(1240, 200), foot(rows(1440, 1), 200, 200**0.5)])

    def fifth(k, count):
        down, at = divmod(60 * k, ROW)
        piece = pltpu.roll(rows(1441 + down, count, 3), (256 - at) % 256, 1) if at else rows(1441 + down, count, 3)
        if at + 60 > ROW:
            more = pltpu.roll(rows(1442 + down, count, 3), ROW - at, 1)
            lanes = lax.broadcasted_iota(jnp.int32, (count, 256), 1)
            piece = jnp.where(lanes < ROW - at, piece, more)
        return piece

    def halves(piece):
        piece = piece[:, :128]
        lanes = lax.broadcasted_iota(jnp.int32, piece.shape, 1)
        return (
            jnp.where(lanes < STOCH, piece, 0.0),
            jnp.where(lanes < STOCH, pltpu.roll(piece, 128 - STOCH, 1), 0.0),
        )

    for k in range(10):
        mean, scale = halves(fifth(k, 20))
        fifth_l[pl.ds(k, 20, stride=10), :] = mean
        fifth_r[pl.ds(k, 20, stride=10), :] = scale
    last_row = rows(1501, 8)
    mean, scale = halves(last_row)
    bias = jnp.concatenate([mean, scale], 1)[0:1]
    w_5[...] = filled([jnp.concatenate([fifth_l[...], fifth_r[...]], 1), foot(bias, 200)])

    def shifted(start, count):
        one = pltpu.roll(rows(start, count), 256 - 60, 1)
        two = pltpu.roll(rows(start + 1, count), ROW - 60, 1)
        lanes = lax.broadcasted_iota(jnp.int32, (count, 256), 1)
        return jnp.where(lanes < ROW - 60, one, jnp.where(lanes < ROW, two, 0.0))

    w_h[:, 768:] = filled([shifted(1501, 200), foot(shifted(1731, 1), 230, 230**0.5)])
    below = shifted(1701, 32)
    below = jnp.where(lax.broadcasted_iota(jnp.int32, (32, 256), 0) < STOCH, below, 0.0)
    w_6z[...] = filled([below], 128)
    last_bias = left[1733:1734, 60:61] * (HOR * bias_scale)
    w_7[...] = jnp.where(row8 == 0, shifted(1732, 1), last_bias)


def prepared(own, other):
    return pl.pallas_call(
        prepare_kernel,
        out_shape=[
            jax.ShapeDtypeStruct((256, 1024), BF16),
            jax.ShapeDtypeStruct((256, 768), BF16),
            jax.ShapeDtypeStruct((128, 256), BF16),
            jax.ShapeDtypeStruct((256, 256), BF16),
            jax.ShapeDtypeStruct((128, 256), BF16),
            jax.ShapeDtypeStruct((256, 256), BF16),
            jax.ShapeDtypeStruct((8, 256), F32),
        ],
        in_specs=[VMEM] * 2,
        out_specs=[VMEM] * 7,
        scratch_shapes=[
            pltpu.VMEM((PEERS, 32, 8, 256), BF16),
            pltpu.VMEM((TABLE, 128), F32),
            pltpu.VMEM((TABLE, 128), F32),
            pltpu.VMEM((200, 128), F32),
            pltpu.VMEM((200, 128), F32),
        ],
        compiler_params=pltpu.CompilerParams(vmem_limit_bytes=40 << 20),
        name="prepare",
    )(own, other)


def from_env(shard):
    start = (lax.axis_index("env") * PEERS + lax.axis_index("cand")) * PART % ROW
    block = lax.dynamic_update_slice(jnp.zeros(8 * ROW, BF16), shard, (start,)).reshape(8, ROW)
    block = jnp.pad(block, ((0, 0), (0, 256 - ROW)))
    return lax.all_to_all(jnp.broadcast_to(block[None], (32, 8, 256)), "env", 0, 0, tiled=True)


def body(params, h_start, z_start, action_noise, state_noise, elites):
    block = from_env(params)
    block, h_start, z_start, action_noise, state_noise, elites = lax.optimization_barrier(
        (block, h_start, z_start, action_noise, state_noise, elites)
    )
    near = [lax.ppermute(block, "cand", [(i, i ^ 2 * k) for i in range(PEERS)]) for k in (1, 2, 3)]
    a_noise = jnp.pad(
        action_noise.reshape(ITERS, HOR, ACT, COLS), ((0, 0), (0, 0), (0, 8 - ACT), (0, 0))
    ).reshape(ITERS, ROWS, COLS)
    s_noise = jnp.pad(
        state_noise.reshape(ITERS, HOR, STOCH, COLS), ((0, 0), (0, 0), (0, 32 - STOCH), (0, 0))
    )

    h0 = jnp.concatenate(
        [h_start, jnp.ones((ENVS_HERE, 2), F32), jnp.zeros((ENVS_HERE, 54), F32)], 1
    )
    z0 = jnp.pad(z_start, ((0, 0), (0, 128 - STOCH)))
    ids = lax.axis_index("cand") * CANDS_HERE + jnp.arange(CANDS_HERE, dtype=jnp.int32)
    chosen = jnp.any(elites[:, :, :, None] == ids, axis=2).astype(F32)

    near, a_noise, s_noise, h0, z0, chosen = lax.optimization_barrier(
        (near, a_noise, s_noise, h0, z0, chosen)
    )
    own = jnp.stack([block, *near])
    other = lax.ppermute(own, "cand", [(i, i ^ 1) for i in range(PEERS)])
    weights = prepared(own, other)
    rets, bests = [], []
    state = got = None
    for number in range(ITERS):
        out = rollout(number, weights, h0, z0, a_noise, s_noise, chosen, state, got)
        rets.append(out[0])
        if number == 0:
            state = jnp.broadcast_to(
                jnp.array([0.0, 1.0, 0.0, 1.0, 0.0, 0.0, 0.0, 0.0], F32)[:, None], (8, 128)
            )
        else:
            state = out[2]
            bests.append(out[3])
        got = lax.all_to_all(out[1], "cand", 0, 0, tiled=True)
    mean, spread, returns, best = pl.pallas_call(
        last_kernel,
        out_shape=[
            jax.ShapeDtypeStruct((ACT, ENVS_HERE, HOR), F32),
            jax.ShapeDtypeStruct((ACT, ENVS_HERE, HOR), F32),
            jax.ShapeDtypeStruct((ITERS, ENVS_HERE, CANDS_HERE), F32),
            jax.ShapeDtypeStruct((ENVS_HERE, ITERS), F32),
        ],
        in_specs=[VMEM] * 7,
        out_specs=[VMEM] * 4,
        compiler_params=pltpu.CompilerParams(vmem_limit_bytes=4 << 20),
        name="last",
    )(state, got, *rets, *bests)
    return mean.transpose(2, 0, 1), spread.transpose(2, 0, 1), returns, best.T


def solution(mesh):
    placed = (
        P(("env", "cand")),
        P("env", None),
        P("env", None),
        P(None, None, None, "env", "cand"),
        P(None, None, None, "env", "cand"),
        P(None, "env", None),
    )
    return jax.shard_map(
        body,
        mesh=mesh,
        in_specs=placed,
        out_specs=(
            P(None, None, "env"),
            P(None, None, "env"),
            P(None, "env", "cand"),
            P(None, "env"),
        ),
        check_vma=False,
    )
```

```python
import functools

import jax
import jax.numpy as jnp
from jax import lax
from jax.experimental import pallas as pl
from jax.experimental.pallas import tpu as pltpu
from jax.sharding import PartitionSpec as P

D_DET = 200
STOCH = 30
HID = 200
ACT = 6
HOR = 12
ITERS = 3

PEERS = 8
ENVS_HERE = 2
CANDS_HERE = 128
COLS = ENVS_HERE * CANDS_HERE

WIDE = 208
DEEP = 256
ROWS = 96
ONE = 96

bias_scale = 0.2
min_scale = 0.1
variance_floor = 1e-05

S36, S400, S200, S230 = (float(n) ** -0.5 for n in (36, 400, 200, 230))
LOG2E = 1.4426950408889634

F32, BF16 = jnp.float32, jnp.bfloat16


def dot(a, b):
    return jnp.dot(a, b, preferred_element_type=F32)


def dot_t(a, b):
    return lax.dot_general(a, b, (((1,), (1,)), ((), ())), preferred_element_type=F32)


def scaled_elu(y, scale):
    return jnp.where(y > 0, y * scale, jnp.exp2(y * (scale * LOG2E)) - 1.0)


def softplus(v):
    return jnp.maximum(v, 0.0) + jnp.log(1.0 + jnp.exp(-jnp.abs(v)))


def refit(state, gathered):
    rows = []
    best = []
    for e in range(ENVS_HERE):
        m1, c1, m2, c2 = (gathered[:, 4 * e + k, :] for k in range(4))
        lowest = c1[:, ONE + 2 : ONE + 3]
        highest = c1[:, ONE + 1 : ONE + 2]
        worst = jnp.min(lowest, axis=0, keepdims=True)
        best.append(jnp.max(highest, axis=0, keepdims=True))
        lift = lowest - worst
        m1 = jnp.sum(m1 + lift * c1, axis=0, keepdims=True)
        m2 = jnp.sum(m2 + lift * c2, axis=0, keepdims=True)
        total = m1[:, ONE : ONE + 1]
        m1 = m1 / total
        m2 = m2 / total
        center = state[2 * e : 2 * e + 1]
        spread = state[2 * e + 1 : 2 * e + 2]
        rows.append(center + spread * m1)
        rows.append(
            jnp.sqrt(spread * spread * jnp.maximum(m2 - m1 * m1, 0.0) + variance_floor)
        )
    state = jnp.concatenate(rows + [jnp.zeros((4, 128), F32)], 0)
    return state, jnp.concatenate([jnp.broadcast_to(b, (1, 128)) for b in best], 0)


def split(v):
    hi = v.astype(BF16)
    return hi, v - hi.astype(F32)


def rollout_kernel(
    first, number, w_h, w_x, w_1, w_5, w_6z, w_r, w_7, h0, z0, a_noise, s_noise, chosen, *rest
):
    if first:
        ret_ref, msg_ref, acts = rest
    else:
        state_ref, got_ref, ret_ref, msg_ref, new_state_ref, best_ref, acts = rest
    noise = a_noise[number].astype(F32)
    if first:
        acts[...] = noise
    else:
        state, best = refit(state_ref[...], got_ref[...])
        new_state_ref[...] = state
        best_ref[...] = best
        columns = jnp.transpose(state)
        for e in range(ENVS_HERE):
            at = pl.ds(e * CANDS_HERE, CANDS_HERE)
            center = columns[:ROWS, 2 * e : 2 * e + 1]
            spread = columns[:ROWS, 2 * e + 1 : 2 * e + 2]
            acts[:, at] = center + spread * noise[:, e * CANDS_HERE : (e + 1) * CANDS_HERE]
    ones8 = jnp.where(lax.broadcasted_iota(jnp.int32, (8, COLS), 0) < 2, 1.0, 0.0).astype(F32)
    filler = jnp.zeros((80, COLS), F32)
    in_latent = lax.broadcasted_iota(jnp.int32, (1, 128), 1) < 32

    def drawn(t, n):
        block = jnp.concatenate([n, acts[t * 8 : t * 8 + 8, :], ones8, filler], 0)
        return jnp.transpose(block)

    def spread_out(ref):
        return jnp.concatenate(
            [jnp.broadcast_to(ref[e : e + 1, :], (CANDS_HERE, ref.shape[1])) for e in range(ENVS_HERE)], 0
        )

    h = spread_out(h0)
    q_sum = None
    for t in range(HOR + 1):
        hd = h.astype(BF16)
        if t == 0:
            za = (spread_out(z0) + drawn(0, jnp.zeros((32, COLS), F32))).astype(BF16)
        else:
            p = scaled_elu(dot(hd, w_h[:, 512:768]), S200).astype(BF16)
            s = dot(p, w_5[...]) * S200
            scale = jnp.where(in_latent, softplus(s[:, 128:]) + min_scale, 1.0)
            n = s_noise[number, t - 1].astype(F32)
            za = (s[:, :128] + scale * drawn(min(t, HOR - 1), n)).astype(BF16)
        if t == HOR:
            q = scaled_elu(dot(hd, w_h[:, 768:]) + dot(za[:, :48], w_6z[:48]), S230)
            q = q.astype(BF16).astype(F32)
            q_sum = q if q_sum is None else q_sum + q
            break
        x = scaled_elu(dot(za[:, :48], w_1[:48]), S36).astype(BF16)
        gates = dot(x, w_x[:, :512]) + dot(hd, w_h[:, :512])
        half = 0.5 * h
        rh = (half + jnp.tanh(gates[:, :256] * (0.5 * S400)) * half).astype(BF16)
        update = 0.5 + 0.5 * jnp.tanh(gates[:, 256:] * (0.5 * S400))
        proposal = jnp.tanh((dot(x, w_x[:, 512:]) + dot(rh, w_r[...])) * S400)
        h = proposal + update * (h - proposal)
        if t > 0:
            q = scaled_elu(dot(hd, w_h[:, 768:]) + dot(za[:, :48], w_6z[:48]), S230)
            q = q.astype(BF16).astype(F32)
            q_sum = q if q_sum is None else q_sum + q

    wide = lax.broadcasted_iota(jnp.int32, (1, COLS), 1)
    wide16 = lax.broadcasted_iota(jnp.int32, (16, COLS), 1) // CANDS_HERE
    rows16 = lax.broadcasted_iota(jnp.int32, (16, COLS), 0)
    lanes = lax.broadcasted_iota(jnp.int32, (1, 128), 1)

    weight = jnp.where(rows16 == 0, w_7[0:1, :], 0.0).astype(BF16)
    part_1, left_over = split(q_sum)
    part_2, left_over = split(left_over)
    r = dot_t(weight, part_1) + (dot_t(weight, part_2) + dot_t(weight, left_over.astype(BF16)))
    n = jnp.concatenate(
        [noise, jnp.where(lax.broadcasted_iota(jnp.int32, (32, COLS), 0) == 0, 1.0, 0.0)], 0
    )
    n2_hi, n2_lo = split(n * n)
    r = r[0:1] * S200 + w_7[1:2, :]
    ends = []
    for e in range(ENVS_HERE):
        mine = r[:, e * CANDS_HERE : (e + 1) * CANDS_HERE]
        ret_ref[e : e + 1, :] = mine
        ends.append((jnp.min(mine, axis=1, keepdims=True), jnp.max(mine, axis=1, keepdims=True)))
    lowest = jnp.where(wide < CANDS_HERE, ends[0][0], ends[1][0])
    c = jnp.concatenate([chosen[number, e : e + 1, :] for e in range(ENVS_HERE)], 1)
    w = c * (r - lowest + 1.0)
    hi, w1 = split(w)
    mid, w2 = split(w1)
    kind = rows16 % 4
    left = jnp.where(
        kind == 0, hi.astype(F32), jnp.where(kind == 1, mid.astype(F32), jnp.where(kind == 2, w2, c))
    )
    left = jnp.where(rows16 // 4 == wide16, left, 0.0).astype(BF16)
    sums = dot_t(left, jnp.concatenate([n.astype(BF16), n2_hi, n2_lo.astype(BF16)], 0))
    first_m, second_m = sums[:8, :128], sums[:8, 128:256] + sums[:8, 256:]
    out = []
    for e in range(ENVS_HERE):
        k = 4 * e
        lowest, highest = ends[e]
        out += [
            first_m[k : k + 1] + first_m[k + 1 : k + 2] + first_m[k + 2 : k + 3],
            jnp.where(
                lanes == ONE + 1, highest, jnp.where(lanes == ONE + 2, lowest, first_m[k + 3 : k + 4])
            ),
            second_m[k : k + 1] + second_m[k + 1 : k + 2] + second_m[k + 2 : k + 3],
            second_m[k + 3 : k + 4],
        ]
    msg = jnp.concatenate(out, 0)
    for k in range(PEERS):
        msg_ref[k] = msg


def last_kernel(
    state_ref, got_ref, r0, r1, r2, b0, b1, mean_ref, spread_ref, ret_ref, best_ref
):
    state, best = refit(state_ref[...], got_ref[...])
    columns = jnp.transpose(state)
    lane = lax.broadcasted_iota(jnp.int32, (8, 128), 1)
    for e in range(ENVS_HERE):
        for ref, k in ((mean_ref, 2 * e), (spread_ref, 2 * e + 1)):
            table = jnp.zeros((8, 128), F32)
            for t in range(HOR):
                table = jnp.where(lane == t, columns[8 * t : 8 * t + 8, k : k + 1], table)
            for a in range(ACT):
                ref[a, e : e + 1, :] = table[a : a + 1, :HOR]
    for i, r in enumerate((r0, r1, r2)):
        ret_ref[i] = r[...]
    lane = lax.broadcasted_iota(jnp.int32, (ENVS_HERE, 128), 1)
    table = jnp.where(lane == 0, b0[...], jnp.where(lane == 1, b1[...], best))
    best_ref[...] = table[:, :ITERS]


VMEM = pl.BlockSpec(memory_space=pltpu.VMEM)


def rollout(number, weights, h0, z0, a_noise, s_noise, chosen, state, got):
    first = state is None
    shapes = [
        jax.ShapeDtypeStruct((ENVS_HERE, CANDS_HERE), F32),
        jax.ShapeDtypeStruct((PEERS, 8, 128), F32),
    ]
    args = [*weights, h0, z0, a_noise, s_noise, chosen]
    if not first:
        shapes += [
            jax.ShapeDtypeStruct((8, 128), F32),
            jax.ShapeDtypeStruct((ENVS_HERE, 128), F32),
        ]
        args += [state, got]
    return pl.pallas_call(
        functools.partial(rollout_kernel, first, number),
        out_shape=shapes,
        in_specs=[VMEM] * len(args),
        out_specs=[VMEM] * len(shapes),
        scratch_shapes=[pltpu.VMEM((ROWS, COLS), F32)],
        compiler_params=pltpu.CompilerParams(vmem_limit_bytes=40 << 20),
        name=f"rollout_{number}",
    )(*args)


PART = 1355
ROW = 200
TABLE = 1752


def prepare_kernel(own, other, w_h, w_x, w_1, w_5, w_6z, w_r, w_7, blocks, left, right, fifth_l, fifth_r):
    here = lax.axis_index("cand")
    y, core = here // 2, here % 2
    for k in range(4):
        there = (y // 2 ^ k // 2) * 2 + (y % 2 ^ k % 2)
        blocks[there * 2 + core] = own[k]
        blocks[there * 2 + 1 - core] = other[k]

    row = lax.broadcasted_iota(jnp.int32, (8, 128), 0)
    lane = lax.broadcasted_iota(jnp.int32, (8, 128), 1)
    for env in range(32):
        for cand in range(PEERS):
            start, first_lane = divmod(PART * (env * PEERS + cand), ROW)
            block = blocks[cand, env].astype(F32)
            for half, table in ((0, left), (1, right)):
                piece = block[:, 128 * half : 128 * half + 128]
                at = table.at[start : start + 8, :]
                if first_lane > 128 * half:
                    mask = (row > 0) | (lane >= first_lane - 128 * half)
                    pltpu.store(at, piece, mask=mask)
                else:
                    at[...] = piece

    def rows(start, count, step=1):
        at = pl.ds(start, count, stride=step) if step > 1 else pl.ds(start, count)
        return jnp.concatenate([left[at, :], right[at, :]], 1)

    row8 = lax.broadcasted_iota(jnp.int32, (8, 256), 0)
    lane8 = lax.broadcasted_iota(jnp.int32, (8, 256), 1)

    def foot(bias, fan_in, ones=0.0):
        bias = jnp.broadcast_to(bias * (bias_scale * fan_in**0.5), (8, 256))
        if ones:
            bias = jnp.where((lane8 == 200) | (lane8 == 201), ones, bias)
        hi = bias.astype(BF16).astype(F32)
        return jnp.where(row8 == 0, hi, jnp.where(row8 == 1, bias - hi, 0.0))

    def filled(parts, count=256):
        used = sum(part.shape[0] for part in parts)
        if used < count:
            parts = [*parts, jnp.zeros((count - used, 256), F32)]
        return jnp.concatenate(parts, 0).astype(BF16)

    first = rows(0, 37)
    state_rows = jnp.where(lax.broadcasted_iota(jnp.int32, (32, 256), 0) < STOCH, first[:32], 0.0)
    action_rows = jnp.where(row8 < ACT, rows(STOCH, 8), 0.0)
    w_1[...] = filled([state_rows, action_rows, foot(rows(36, 1), 36, 6.0)], 128)
    w_x[:, :256] = filled([rows(37, 200, 2), foot(rows(837, 1), 400)])
    w_x[:, 256:512] = filled([rows(38, 200, 2), foot(rows(838, 1), 400, 2000.0)])
    w_h[:, :256] = filled([rows(437, 200, 2)])
    w_h[:, 256:512] = filled([rows(438, 200, 2)])
    w_x[:, 512:] = filled([rows(839, 200), foot(rows(1239, 1), 400)])
    w_r[...] = filled([rows(1039, 200)])
    w_h[:, 512:768] = filled([rows(1240, 200), foot(rows(1440, 1), 200, 200**0.5)])

    def fifth(k, count):
        down, at = divmod(60 * k, ROW)
        piece = pltpu.roll(rows(1441 + down, count, 3), (256 - at) % 256, 1) if at else rows(1441 + down, count, 3)
        if at + 60 > ROW:
            more = pltpu.roll(rows(1442 + down, count, 3), ROW - at, 1)
            lanes = lax.broadcasted_iota(jnp.int32, (count, 256), 1)
            piece = jnp.where(lanes < ROW - at, piece, more)
        return piece

    def halves(piece):
        piece = piece[:, :128]
        lanes = lax.broadcasted_iota(jnp.int32, piece.shape, 1)
        return (
            jnp.where(lanes < STOCH, piece, 0.0),
            jnp.where(lanes < STOCH, pltpu.roll(piece, 128 - STOCH, 1), 0.0),
        )

    for k in range(10):
        mean, scale = halves(fifth(k, 20))
        fifth_l[pl.ds(k, 20, stride=10), :] = mean
        fifth_r[pl.ds(k, 20, stride=10), :] = scale
    last_row = rows(1501, 8)
    mean, scale = halves(last_row)
    bias = jnp.concatenate([mean, scale], 1)[0:1]
    w_5[...] = filled([jnp.concatenate([fifth_l[:200], fifth_r[:200]], 1), foot(bias, 200)])

    def shifted(start, count):
        one = pltpu.roll(rows(start, count), 256 - 60, 1)
        two = pltpu.roll(rows(start + 1, count), ROW - 60, 1)
        lanes = lax.broadcasted_iota(jnp.int32, (count, 256), 1)
        return jnp.where(lanes < ROW - 60, one, jnp.where(lanes < ROW, two, 0.0))

    w_h[:, 768:] = filled([shifted(1501, 200), foot(shifted(1731, 1), 230, 230**0.5)])
    below = shifted(1701, 32)
    below = jnp.where(lax.broadcasted_iota(jnp.int32, (32, 256), 0) < STOCH, below, 0.0)
    w_6z[...] = filled([below], 128)
    last_bias = left[1733:1734, 60:61] * (HOR * bias_scale)
    w_7[...] = jnp.where(row8 == 0, shifted(1732, 1), last_bias)


def prepared(own, other):
    return pl.pallas_call(
        prepare_kernel,
        out_shape=[
            jax.ShapeDtypeStruct((256, 1024), BF16),
            jax.ShapeDtypeStruct((256, 768), BF16),
            jax.ShapeDtypeStruct((128, 256), BF16),
            jax.ShapeDtypeStruct((256, 256), BF16),
            jax.ShapeDtypeStruct((128, 256), BF16),
            jax.ShapeDtypeStruct((256, 256), BF16),
            jax.ShapeDtypeStruct((8, 256), F32),
        ],
        in_specs=[VMEM] * 2,
        out_specs=[VMEM] * 7,
        scratch_shapes=[
            pltpu.VMEM((PEERS, 32, 8, 256), BF16),
            pltpu.VMEM((TABLE, 128), F32),
            pltpu.VMEM((TABLE, 128), F32),
            pltpu.VMEM((256, 128), F32),
            pltpu.VMEM((256, 128), F32),
        ],
        compiler_params=pltpu.CompilerParams(vmem_limit_bytes=40 << 20),
        name="prepare",
    )(own, other)


def from_env(shard):
    start = (lax.axis_index("env") * PEERS + lax.axis_index("cand")) * PART % ROW
    block = lax.dynamic_update_slice(jnp.zeros(8 * ROW, BF16), shard, (start,)).reshape(8, ROW)
    block = jnp.pad(block, ((0, 0), (0, 256 - ROW)))
    return lax.all_to_all(jnp.broadcast_to(block[None], (32, 8, 256)), "env", 0, 0, tiled=True)


def body(params, h_start, z_start, action_noise, state_noise, elites):
    block = from_env(params)
    block, h_start, z_start, action_noise, state_noise, elites = lax.optimization_barrier(
        (block, h_start, z_start, action_noise, state_noise, elites)
    )
    near = [lax.ppermute(block, "cand", [(i, i ^ 2 * k) for i in range(PEERS)]) for k in (1, 2, 3)]
    a_noise = jnp.pad(
        action_noise.reshape(ITERS, HOR, ACT, COLS), ((0, 0), (0, 0), (0, 8 - ACT), (0, 0))
    ).reshape(ITERS, ROWS, COLS)
    s_noise = jnp.pad(
        state_noise.reshape(ITERS, HOR, STOCH, COLS), ((0, 0), (0, 0), (0, 32 - STOCH), (0, 0))
    )

    h0 = jnp.concatenate(
        [h_start, jnp.ones((ENVS_HERE, 2), F32), jnp.zeros((ENVS_HERE, 54), F32)], 1
    )
    z0 = jnp.pad(z_start, ((0, 0), (0, 128 - STOCH)))
    ids = lax.axis_index("cand") * CANDS_HERE + jnp.arange(CANDS_HERE, dtype=jnp.int32)
    chosen = jnp.any(elites[:, :, :, None] == ids, axis=2).astype(F32)

    near, a_noise, s_noise, h0, z0, chosen = lax.optimization_barrier(
        (near, a_noise, s_noise, h0, z0, chosen)
    )
    own = jnp.stack([block, *near])
    other = lax.ppermute(own, "cand", [(i, i ^ 1) for i in range(PEERS)])
    weights = prepared(own, other)
    rets, bests = [], []
    state = got = None
    for number in range(ITERS):
        out = rollout(number, weights, h0, z0, a_noise, s_noise, chosen, state, got)
        rets.append(out[0])
        if number == 0:
            state = jnp.broadcast_to(
                jnp.array([0.0, 1.0, 0.0, 1.0, 0.0, 0.0, 0.0, 0.0], F32)[:, None], (8, 128)
            )
        else:
            state = out[2]
            bests.append(out[3])
        got = lax.all_to_all(out[1], "cand", 0, 0, tiled=True)
    mean, spread, returns, best = pl.pallas_call(
        last_kernel,
        out_shape=[
            jax.ShapeDtypeStruct((ACT, ENVS_HERE, HOR), F32),
            jax.ShapeDtypeStruct((ACT, ENVS_HERE, HOR), F32),
            jax.ShapeDtypeStruct((ITERS, ENVS_HERE, CANDS_HERE), F32),
            jax.ShapeDtypeStruct((ENVS_HERE, ITERS), F32),
        ],
        in_specs=[VMEM] * 7,
        out_specs=[VMEM] * 4,
        compiler_params=pltpu.CompilerParams(vmem_limit_bytes=4 << 20),
        name="last",
    )(state, got, *rets, *bests)
    return mean.transpose(2, 0, 1), spread.transpose(2, 0, 1), returns, best.T


def solution(mesh):
    placed = (
        P(("env", "cand")),
        P("env", None),
        P("env", None),
        P(None, None, None, "env", "cand"),
        P(None, None, None, "env", "cand"),
        P(None, "env", None),
    )
    return jax.shard_map(
        body,
        mesh=mesh,
        in_specs=placed,
        out_specs=(
            P(None, None, "env"),
            P(None, None, "env"),
            P(None, "env", "cand"),
            P(None, "env"),
        ),
        check_vma=False,
    )
```

```python
import functools

import jax
import jax.numpy as jnp
from jax import lax
from jax.experimental import pallas as pl
from jax.experimental.pallas import tpu as pltpu
from jax.sharding import PartitionSpec as P

D_DET = 200
STOCH = 30
HID = 200
ACT = 6
HOR = 12
ITERS = 3

PEERS = 8
ENVS_HERE = 2
CANDS_HERE = 128
COLS = ENVS_HERE * CANDS_HERE

WIDE = 208
DEEP = 256
ROWS = 96
ONE = 96

bias_scale = 0.2
min_scale = 0.1
variance_floor = 1e-05

S36, S400, S200, S230 = (float(n) ** -0.5 for n in (36, 400, 200, 230))
LOG2E = 1.4426950408889634

F32, BF16 = jnp.float32, jnp.bfloat16


def dot(a, b):
    return jnp.dot(a, b, preferred_element_type=F32)


def dot_t(a, b):
    return lax.dot_general(a, b, (((1,), (1,)), ((), ())), preferred_element_type=F32)


def scaled_elu(y, scale):
    return jnp.where(y > 0, y * scale, jnp.exp2(y * (scale * LOG2E)) - 1.0)


def softplus(v):
    return jnp.maximum(v, 0.0) + jnp.log(1.0 + jnp.exp(-jnp.abs(v)))


def refit(state, gathered):
    rows = []
    best = []
    for e in range(ENVS_HERE):
        m1, c1, m2, c2 = (gathered[:, 4 * e + k, :] for k in range(4))
        lowest = c1[:, ONE + 2 : ONE + 3]
        highest = c1[:, ONE + 1 : ONE + 2]
        worst = jnp.min(lowest, axis=0, keepdims=True)
        best.append(jnp.max(highest, axis=0, keepdims=True))
        lift = lowest - worst
        m1 = jnp.sum(m1 + lift * c1, axis=0, keepdims=True)
        m2 = jnp.sum(m2 + lift * c2, axis=0, keepdims=True)
        total = m1[:, ONE : ONE + 1]
        m1 = m1 / total
        m2 = m2 / total
        center = state[2 * e : 2 * e + 1]
        spread = state[2 * e + 1 : 2 * e + 2]
        rows.append(center + spread * m1)
        rows.append(
            jnp.sqrt(spread * spread * jnp.maximum(m2 - m1 * m1, 0.0) + variance_floor)
        )
    state = jnp.concatenate(rows + [jnp.zeros((4, 128), F32)], 0)
    return state, jnp.concatenate([jnp.broadcast_to(b, (1, 128)) for b in best], 0)


def split(v):
    hi = v.astype(BF16)
    return hi, v - hi.astype(F32)


def rollout_kernel(
    first, number, w_h, w_x, w_1, w_5, w_6z, w_r, w_7, h0, z0, a_noise, s_noise, chosen, *rest
):
    if first:
        ret_ref, msg_ref, acts = rest
    else:
        state_ref, got_ref, ret_ref, msg_ref, new_state_ref, best_ref, acts = rest
    noise = a_noise[number].astype(F32)
    if first:
        acts[...] = noise
    else:
        state, best = refit(state_ref[...], got_ref[...])
        new_state_ref[...] = state
        best_ref[...] = best
        columns = jnp.transpose(state)
        for e in range(ENVS_HERE):
            at = pl.ds(e * CANDS_HERE, CANDS_HERE)
            center = columns[:ROWS, 2 * e : 2 * e + 1]
            spread = columns[:ROWS, 2 * e + 1 : 2 * e + 2]
            acts[:, at] = center + spread * noise[:, e * CANDS_HERE : (e + 1) * CANDS_HERE]
    ones8 = jnp.where(lax.broadcasted_iota(jnp.int32, (8, COLS), 0) < 2, 1.0, 0.0).astype(F32)
    filler = jnp.zeros((80, COLS), F32)
    in_latent = lax.broadcasted_iota(jnp.int32, (1, 128), 1) < 32

    def drawn(t, n):
        block = jnp.concatenate([n, acts[t * 8 : t * 8 + 8, :], ones8, filler], 0)
        return jnp.transpose(block)

    def spread_out(ref):
        return jnp.concatenate(
            [jnp.broadcast_to(ref[e : e + 1, :], (CANDS_HERE, ref.shape[1])) for e in range(ENVS_HERE)], 0
        )

    h = spread_out(h0)
    q_sum = None
    for t in range(HOR + 1):
        hd = h.astype(BF16)
        if t == 0:
            za = (spread_out(z0) + drawn(0, jnp.zeros((32, COLS), F32))).astype(BF16)
        else:
            p = scaled_elu(dot(hd, w_h[:, 512:768]), S200).astype(BF16)
            s = dot(p, w_5[...]) * S200
            scale = jnp.where(in_latent, softplus(s[:, 128:]) + min_scale, 1.0)
            n = s_noise[number, t - 1].astype(F32)
            za = (s[:, :128] + scale * drawn(min(t, HOR - 1), n)).astype(BF16)
        if t == HOR:
            q = scaled_elu(dot(hd, w_h[:, 768:]) + dot(za[:, :48], w_6z[:48]), S230)
            q = q.astype(BF16).astype(F32)
            q_sum = q if q_sum is None else q_sum + q
            break
        x = scaled_elu(dot(za[:, :48], w_1[:48]), S36).astype(BF16)
        gates = dot(x, w_x[:, :512]) + dot(hd, w_h[:, :512])
        half = 0.5 * h
        rh = (half + jnp.tanh(gates[:, :256] * (0.5 * S400)) * half).astype(BF16)
        proposal = jnp.tanh((dot(x, w_x[:, 512:]) + dot(rh, w_r[...])) * S400)
        update = 0.5 + 0.5 * jnp.tanh(gates[:, 256:] * (0.5 * S400))
        h = proposal + update * (h - proposal)
        if t > 0:
            q = scaled_elu(dot(hd, w_h[:, 768:]) + dot(za[:, :48], w_6z[:48]), S230)
            q = q.astype(BF16).astype(F32)
            q_sum = q if q_sum is None else q_sum + q

    wide = lax.broadcasted_iota(jnp.int32, (1, COLS), 1)
    wide16 = lax.broadcasted_iota(jnp.int32, (16, COLS), 1) // CANDS_HERE
    rows16 = lax.broadcasted_iota(jnp.int32, (16, COLS), 0)
    lanes = lax.broadcasted_iota(jnp.int32, (1, 128), 1)

    weight = jnp.where(rows16 == 0, w_7[0:1, :], 0.0).astype(BF16)
    part_1, left_over = split(q_sum)
    part_2, left_over = split(left_over)
    r = dot_t(weight, part_1) + (dot_t(weight, part_2) + dot_t(weight, left_over.astype(BF16)))
    n = jnp.concatenate(
        [noise, jnp.where(lax.broadcasted_iota(jnp.int32, (32, COLS), 0) == 0, 1.0, 0.0)], 0
    )
    n2_hi, n2_lo = split(n * n)
    r = r[0:1] * S200 + w_7[1:2, :]
    ends = []
    for e in range(ENVS_HERE):
        mine = r[:, e * CANDS_HERE : (e + 1) * CANDS_HERE]
        ret_ref[e : e + 1, :] = mine
        ends.append((jnp.min(mine, axis=1, keepdims=True), jnp.max(mine, axis=1, keepdims=True)))
    lowest = jnp.where(wide < CANDS_HERE, ends[0][0], ends[1][0])
    c = jnp.concatenate([chosen[number, e : e + 1, :] for e in range(ENVS_HERE)], 1)
    w = c * (r - lowest + 1.0)
    hi, w1 = split(w)
    mid, w2 = split(w1)
    kind = rows16 % 4
    left = jnp.where(
        kind == 0, hi.astype(F32), jnp.where(kind == 1, mid.astype(F32), jnp.where(kind == 2, w2, c))
    )
    left = jnp.where(rows16 // 4 == wide16, left, 0.0).astype(BF16)
    sums = dot_t(left, jnp.concatenate([n.astype(BF16), n2_hi, n2_lo.astype(BF16)], 0))
    first_m, second_m = sums[:8, :128], sums[:8, 128:256] + sums[:8, 256:]
    out = []
    for e in range(ENVS_HERE):
        k = 4 * e
        lowest, highest = ends[e]
        out += [
            first_m[k : k + 1] + first_m[k + 1 : k + 2] + first_m[k + 2 : k + 3],
            jnp.where(
                lanes == ONE + 1, highest, jnp.where(lanes == ONE + 2, lowest, first_m[k + 3 : k + 4])
            ),
            second_m[k : k + 1] + second_m[k + 1 : k + 2] + second_m[k + 2 : k + 3],
            second_m[k + 3 : k + 4],
        ]
    msg = jnp.concatenate(out, 0)
    for k in range(PEERS):
        msg_ref[k] = msg


def last_kernel(
    state_ref, got_ref, r0, r1, r2, b0, b1, mean_ref, spread_ref, ret_ref, best_ref
):
    state, best = refit(state_ref[...], got_ref[...])
    columns = jnp.transpose(state)
    lane = lax.broadcasted_iota(jnp.int32, (8, 128), 1)
    for e in range(ENVS_HERE):
        for ref, k in ((mean_ref, 2 * e), (spread_ref, 2 * e + 1)):
            table = jnp.zeros((8, 128), F32)
            for t in range(HOR):
                table = jnp.where(lane == t, columns[8 * t : 8 * t + 8, k : k + 1], table)
            for a in range(ACT):
                ref[a, e : e + 1, :] = table[a : a + 1, :HOR]
    for i, r in enumerate((r0, r1, r2)):
        ret_ref[i] = r[...]
    lane = lax.broadcasted_iota(jnp.int32, (ENVS_HERE, 128), 1)
    table = jnp.where(lane == 0, b0[...], jnp.where(lane == 1, b1[...], best))
    best_ref[...] = table[:, :ITERS]


VMEM = pl.BlockSpec(memory_space=pltpu.VMEM)


def rollout(number, weights, h0, z0, a_noise, s_noise, chosen, state, got):
    first = state is None
    shapes = [
        jax.ShapeDtypeStruct((ENVS_HERE, CANDS_HERE), F32),
        jax.ShapeDtypeStruct((PEERS, 8, 128), F32),
    ]
    args = [*weights, h0, z0, a_noise, s_noise, chosen]
    if not first:
        shapes += [
            jax.ShapeDtypeStruct((8, 128), F32),
            jax.ShapeDtypeStruct((ENVS_HERE, 128), F32),
        ]
        args += [state, got]
    return pl.pallas_call(
        functools.partial(rollout_kernel, first, number),
        out_shape=shapes,
        in_specs=[VMEM] * len(args),
        out_specs=[VMEM] * len(shapes),
        scratch_shapes=[pltpu.VMEM((ROWS, COLS), F32)],
        compiler_params=pltpu.CompilerParams(vmem_limit_bytes=40 << 20),
        name=f"rollout_{number}",
    )(*args)


PART = 1355
ROW = 200
TABLE = 1752


def prepare_kernel(own, other, w_h, w_x, w_1, w_5, w_6z, w_r, w_7, blocks, left, right, fifth_l, fifth_r):
    here = lax.axis_index("cand")
    y, core = here // 2, here % 2
    for k in range(4):
        there = (y // 2 ^ k // 2) * 2 + (y % 2 ^ k % 2)
        blocks[there * 2 + core] = own[k]
        blocks[there * 2 + 1 - core] = other[k]

    row = lax.broadcasted_iota(jnp.int32, (8, 128), 0)
    lane = lax.broadcasted_iota(jnp.int32, (8, 128), 1)
    for env in range(32):
        for cand in range(PEERS):
            start, first_lane = divmod(PART * (env * PEERS + cand), ROW)
            block = blocks[cand, env].astype(F32)
            for half, table in ((0, left), (1, right)):
                piece = block[:, 128 * half : 128 * half + 128]
                at = table.at[start : start + 8, :]
                if first_lane > 128 * half:
                    mask = (row > 0) | (lane >= first_lane - 128 * half)
                    pltpu.store(at, piece, mask=mask)
                else:
                    at[...] = piece

    def rows(start, count, step=1):
        at = pl.ds(start, count, stride=step) if step > 1 else pl.ds(start, count)
        return jnp.concatenate([left[at, :], right[at, :]], 1)

    row8 = lax.broadcasted_iota(jnp.int32, (8, 256), 0)
    lane8 = lax.broadcasted_iota(jnp.int32, (8, 256), 1)

    def foot(bias, fan_in, ones=0.0):
        bias = jnp.broadcast_to(bias * (bias_scale * fan_in**0.5), (8, 256))
        if ones:
            bias = jnp.where((lane8 == 200) | (lane8 == 201), ones, bias)
        hi = bias.astype(BF16).astype(F32)
        return jnp.where(row8 == 0, hi, jnp.where(row8 == 1, bias - hi, 0.0))

    def filled(parts, count=256):
        used = sum(part.shape[0] for part in parts)
        if used < count:
            parts = [*parts, jnp.zeros((count - used, 256), F32)]
        return jnp.concatenate(parts, 0).astype(BF16)

    first = rows(0, 37)
    state_rows = jnp.where(lax.broadcasted_iota(jnp.int32, (32, 256), 0) < STOCH, first[:32], 0.0)
    action_rows = jnp.where(row8 < ACT, rows(STOCH, 8), 0.0)
    w_1[...] = filled([state_rows, action_rows, foot(rows(36, 1), 36, 6.0)], 128)
    w_x[:, :256] = filled([rows(37, 200, 2), foot(rows(837, 1), 400)])
    w_x[:, 256:512] = filled([rows(38, 200, 2), foot(rows(838, 1), 400, 2000.0)])
    w_h[:, :256] = filled([rows(437, 200, 2)])
    w_h[:, 256:512] = filled([rows(438, 200, 2)])
    w_x[:, 512:] = filled([rows(839, 200), foot(rows(1239, 1), 400)])
    w_r[...] = filled([rows(1039, 200)])
    w_h[:, 512:768] = filled([rows(1240, 200), foot(rows(1440, 1), 200, 200**0.5)])

    def fifth(k, count):
        down, at = divmod(60 * k, ROW)
        piece = pltpu.roll(rows(1441 + down, count, 3), (256 - at) % 256, 1) if at else rows(1441 + down, count, 3)
        if at + 60 > ROW:
            more = pltpu.roll(rows(1442 + down, count, 3), ROW - at, 1)
            lanes = lax.broadcasted_iota(jnp.int32, (count, 256), 1)
            piece = jnp.where(lanes < ROW - at, piece, more)
        return piece

    def halves(piece):
        piece = piece[:, :128]
        lanes = lax.broadcasted_iota(jnp.int32, piece.shape, 1)
        return (
            jnp.where(lanes < STOCH, piece, 0.0),
            jnp.where(lanes < STOCH, pltpu.roll(piece, 128 - STOCH, 1), 0.0),
        )

    for k in range(10):
        mean, scale = halves(fifth(k, 20))
        fifth_l[pl.ds(k, 20, stride=10), :] = mean
        fifth_r[pl.ds(k, 20, stride=10), :] = scale
    last_row = rows(1501, 8)
    mean, scale = halves(last_row)
    bias = jnp.concatenate([mean, scale], 1)[0:1]
    w_5[...] = filled([jnp.concatenate([fifth_l[:200], fifth_r[:200]], 1), foot(bias, 200)])

    def shifted(start, count):
        one = pltpu.roll(rows(start, count), 256 - 60, 1)
        two = pltpu.roll(rows(start + 1, count), ROW - 60, 1)
        lanes = lax.broadcasted_iota(jnp.int32, (count, 256), 1)
        return jnp.where(lanes < ROW - 60, one, jnp.where(lanes < ROW, two, 0.0))

    w_h[:, 768:] = filled([shifted(1501, 200), foot(shifted(1731, 1), 230, 230**0.5)])
    below = shifted(1701, 32)
    below = jnp.where(lax.broadcasted_iota(jnp.int32, (32, 256), 0) < STOCH, below, 0.0)
    w_6z[...] = filled([below], 128)
    last_bias = left[1733:1734, 60:61] * (HOR * bias_scale)
    w_7[...] = jnp.where(row8 == 0, shifted(1732, 1), last_bias)


def prepared(own, other):
    return pl.pallas_call(
        prepare_kernel,
        out_shape=[
            jax.ShapeDtypeStruct((256, 1024), BF16),
            jax.ShapeDtypeStruct((256, 768), BF16),
            jax.ShapeDtypeStruct((128, 256), BF16),
            jax.ShapeDtypeStruct((256, 256), BF16),
            jax.ShapeDtypeStruct((128, 256), BF16),
            jax.ShapeDtypeStruct((256, 256), BF16),
            jax.ShapeDtypeStruct((8, 256), F32),
        ],
        in_specs=[VMEM] * 2,
        out_specs=[VMEM] * 7,
        scratch_shapes=[
            pltpu.VMEM((PEERS, 32, 8, 256), BF16),
            pltpu.VMEM((TABLE, 128), F32),
            pltpu.VMEM((TABLE, 128), F32),
            pltpu.VMEM((256, 128), F32),
            pltpu.VMEM((256, 128), F32),
        ],
        compiler_params=pltpu.CompilerParams(vmem_limit_bytes=40 << 20),
        name="prepare",
    )(own, other)


def from_env(shard):
    start = (lax.axis_index("env") * PEERS + lax.axis_index("cand")) * PART % ROW
    block = lax.dynamic_update_slice(jnp.zeros(8 * ROW, BF16), shard, (start,)).reshape(8, ROW)
    block = jnp.pad(block, ((0, 0), (0, 256 - ROW)))
    return lax.all_to_all(jnp.broadcast_to(block[None], (32, 8, 256)), "env", 0, 0, tiled=True)


def body(params, h_start, z_start, action_noise, state_noise, elites):
    block = from_env(params)
    block, h_start, z_start, action_noise, state_noise, elites = lax.optimization_barrier(
        (block, h_start, z_start, action_noise, state_noise, elites)
    )
    near = [lax.ppermute(block, "cand", [(i, i ^ 2 * k) for i in range(PEERS)]) for k in (1, 2, 3)]
    a_noise = jnp.pad(
        action_noise.reshape(ITERS, HOR, ACT, COLS), ((0, 0), (0, 0), (0, 8 - ACT), (0, 0))
    ).reshape(ITERS, ROWS, COLS)
    s_noise = jnp.pad(
        state_noise.reshape(ITERS, HOR, STOCH, COLS), ((0, 0), (0, 0), (0, 32 - STOCH), (0, 0))
    )

    h0 = jnp.concatenate(
        [h_start, jnp.ones((ENVS_HERE, 2), F32), jnp.zeros((ENVS_HERE, 54), F32)], 1
    )
    z0 = jnp.pad(z_start, ((0, 0), (0, 128 - STOCH)))
    ids = lax.axis_index("cand") * CANDS_HERE + jnp.arange(CANDS_HERE, dtype=jnp.int32)
    chosen = jnp.any(elites[:, :, :, None] == ids, axis=2).astype(F32)

    near, a_noise, s_noise, h0, z0, chosen = lax.optimization_barrier(
        (near, a_noise, s_noise, h0, z0, chosen)
    )
    own = jnp.stack([block, *near])
    other = lax.ppermute(own, "cand", [(i, i ^ 1) for i in range(PEERS)])
    weights = prepared(own, other)
    rets, bests = [], []
    state = got = None
    for number in range(ITERS):
        out = rollout(number, weights, h0, z0, a_noise, s_noise, chosen, state, got)
        rets.append(out[0])
        if number == 0:
            state = jnp.broadcast_to(
                jnp.array([0.0, 1.0, 0.0, 1.0, 0.0, 0.0, 0.0, 0.0], F32)[:, None], (8, 128)
            )
        else:
            state = out[2]
            bests.append(out[3])
        got = lax.all_to_all(out[1], "cand", 0, 0, tiled=True)
    mean, spread, returns, best = pl.pallas_call(
        last_kernel,
        out_shape=[
            jax.ShapeDtypeStruct((ACT, ENVS_HERE, HOR), F32),
            jax.ShapeDtypeStruct((ACT, ENVS_HERE, HOR), F32),
            jax.ShapeDtypeStruct((ITERS, ENVS_HERE, CANDS_HERE), F32),
            jax.ShapeDtypeStruct((ENVS_HERE, ITERS), F32),
        ],
        in_specs=[VMEM] * 7,
        out_specs=[VMEM] * 4,
        compiler_params=pltpu.CompilerParams(vmem_limit_bytes=4 << 20),
        name="last",
    )(state, got, *rets, *bests)
    return mean.transpose(2, 0, 1), spread.transpose(2, 0, 1), returns, best.T


def solution(mesh):
    placed = (
        P(("env", "cand")),
        P("env", None),
        P("env", None),
        P(None, None, None, "env", "cand"),
        P(None, None, None, "env", "cand"),
        P(None, "env", None),
    )
    return jax.shard_map(
        body,
        mesh=mesh,
        in_specs=placed,
        out_specs=(
            P(None, None, "env"),
            P(None, None, "env"),
            P(None, "env", "cand"),
            P(None, "env"),
        ),
        check_vma=False,
    )
```
